256 devices in a mesh: stream: 8 (over z), mod: 32 (over y, x, core).
Axes of the slice: x: 4, y: 4, z: 8, core: 2. Of those that a mesh axis runs over, the one named last changes fastest.
Arguments:
- pixels: bfloat16 [8, 768, 512, 384], P('stream', None, 'mod'), may hold values from -6 to 6
- stem_weight: bfloat16 [256, 128], replicated, may hold values from -0.375 to 0.375
- veto_weight: float32 [32, 128], replicated, may hold values from -0.25 to 0.25
- hit_frames: int32 [8, 192], P('stream'), may hold values from 0 to 767, as said below
- assign: int32 [8, 192, 1], P('stream'), may hold values from 0 to 7; in each aligned block of 6 rows (0 to 5, 6 to 11, ..., all dimensions but the last counted through in order) at most 2 rows name the same one
- token_in: bfloat16 [8, 384, 24], P('stream'), may hold values from -1.25 to 1.25
- token_out: bfloat16 [8, 24, 384], P('stream'), may hold values from -0.3125 to 0.3125
- chan_in: bfloat16 [8, 128, 512], P('stream'), may hold values from -0.5 to 0.5
- chan_out: bfloat16 [8, 512, 128], P('stream'), may hold values from -0.25 to 0.25
- readout: bfloat16 [4096, 128], replicated, may hold values from -0.09375 to 0.09375
- latent_gain: float32 [128], replicated, may hold values from 0.1 to 1.9
- class_weight: float32 [128, 8], replicated, may hold values from -0.5 to 0.5
Outputs:
- veto: float32 [8, 768], P('stream', 'mod')
- latents: float32 [8, 192, 128], P('stream', 'mod')
- scores: float32 [8, 192, 8], P('stream', 'mod')
The draws below stay inside these ranges and needn't reach their ends.
Inputs may be any that keep to these rules, and one draw needn't show every extreme that they name: `hit_frames`: each row lists, rising and distinct, exactly 6 frames from every aligned block of 24 frames. `assign`: within the 6 hits of one aligned block (one owner's hits) no stream is named more than 2 times.
All inputs are finite; a program needn't handle non-finite values.
Results may differ from the reference program's by a relative error of at most 0.0095.
Values may be sent and summed in bfloat16 or wider, within the bound.
A program may use at most 128 MiB of HBM per device.

```python
import math
import jax
import jax.numpy as jnp
import numpy as np
from jax import lax

C = 128
TMIX = 384
HID = 512
NCLS = 8
PATCH = 16
ROWS_DEV = 16
COLS = 384
FR_DEV = 24
CAP = 2
WT = 24
FRAMES = 768
HIT_DEV = 6
HITS = 192
N_STREAM = 8
N_MOD = 32


def draw_hit_frames(key, part):
    owners = FRAMES // FR_DEV
    n_blocks = N_STREAM * owners
    random_keys = jax.random.randint(key, (n_blocks, FR_DEV), 0, 2 ** 20)
    distinct = random_keys * FR_DEV + jnp.arange(FR_DEV, dtype=jnp.int32)[None, :]
    picked = jnp.sort(jnp.argsort(distinct, axis=1)[:, :HIT_DEV].astype(jnp.int32), axis=1)
    offsets = jnp.arange(n_blocks, dtype=jnp.int32) % owners * FR_DEV
    return (picked + offsets[:, None]).astype(jnp.int32).reshape(N_STREAM, HITS)


def steps_of(key, extent, shards, smallest, largest):
    loudness, own = 1.0, jax.random.fold_in(key, 6)
    for axis_at, blocks in shards:
        steps = jnp.exp(jax.random.uniform(jax.random.fold_in(own, axis_at), (blocks,), jnp.float32, smallest / len(shards), largest / len(shards)))
        loudness = loudness * jnp.repeat(steps, extent[axis_at] // blocks).reshape([-1 if axis == axis_at else 1 for axis in range(len(extent))])
    return loudness


def routed_block(rng, own, number, rows, count, top, limit, slope):
    sequence = jax.random.permutation(rng, count)
    crowded, common = load_shares(count, rows * top, limit, slope, True), load_shares(count, rows * top, limit, slope, False)
    places = jnp.arange(count)

    def named(sizes, turn):
        used = int((sizes > 0).sum())
        fixed = max(1, used // 4)
        shifted = fixed + (places - fixed + turn * (used - fixed)) % max(1, count - fixed)
        return jnp.zeros((count,), jnp.int32).at[sequence[jnp.where(places < fixed, places, shifted)]].set(jnp.asarray(sizes, jnp.int32))

    sizes = jnp.where(number % 4 == 0, named(crowded, number // 4), named(common, number - number // 4 - 1))
    mixed = jax.random.permutation(jax.random.fold_in(own, 3), count)
    donor, sink = mixed[0:count // 2 * 2:2], mixed[1:count // 2 * 2:2]
    slack = jnp.minimum(sizes[donor] - 1, limit - sizes[sink]) // 2
    slack = jnp.where((donor == sequence[0]) | (sink == sequence[0]) | (sizes[sink] == 0), 0, jnp.maximum(slack, 0))
    shifted = jax.random.randint(jax.random.fold_in(own, 4), (count // 2,), 0, 1 << 20) % (slack + 1)
    sizes = sizes.at[donor].add(-shifted).at[sink].add(shifted)
    members = jnp.searchsorted(jnp.cumsum(sizes), jnp.arange(rows * top), side="right").astype(jnp.int32)
    grid = members.reshape(top, rows).T
    grid = grid[jax.random.permutation(jax.random.fold_in(own, 1), rows)]
    turn = jax.random.randint(jax.random.fold_in(own, 2), (rows, 1), 0, top)
    return jnp.take_along_axis(grid, (jnp.arange(top)[None, :] + turn) % top, axis=1)


def load_shares(count, total, reach, slope, full):
    portions = [(1 << 20) // math.isqrt(standing ** slope) + 1 for standing in range(1, count + 1)]
    largest = reach if full else min(reach, max(-(-total // count), total * portions[0] // sum(portions)))
    least = 1 if total - largest >= count - 1 else 0
    holding, surplus = [largest] + [least] * (count - 1), total - largest - least * (count - 1)
    while surplus > 0:
        free = [i for i in range(1, count) if holding[i] < largest] or [i for i in range(1, count) if holding[i] < reach]
        whole, budget = sum([portions[i] for i in free]), surplus
        for i in free:
            extra = min(reach - holding[i], max(1, budget * portions[i] // whole), surplus)
            holding[i] = holding[i] + extra
            surplus = surplus - extra
    return np.array(holding)


def bell_draw(own_key, shape, spread, limit, shards=(), kind=jnp.bfloat16):
    entries = spread * jax.random.normal(own_key, shape, jnp.float32)
    if shards:
        entries = entries * steps_of(own_key, shape, shards, -0.22, 0.18)
    return jnp.clip(entries, -limit, limit).astype(kind)


def setup_inputs(seed: int = 0) -> dict:
    arg_keys = jax.random.split(jax.random.key(seed), 13)
    pixels = bell_draw(arg_keys[0], (N_STREAM, FRAMES, N_MOD * ROWS_DEV, COLS), 1.0, 6.0, ((0, 8), (2, 32)))
    stem_weight = bell_draw(arg_keys[1], (PATCH * PATCH, C), (PATCH * PATCH) ** -0.5, 0.375)
    veto_weight = bell_draw(arg_keys[2], (N_MOD, C), (4 * C) ** -0.5, 0.25, (), jnp.float32)
    hit_frames = draw_hit_frames(jax.random.fold_in(arg_keys[12], 71), 0)
    assign_keys = jax.random.split(jax.random.fold_in(arg_keys[4], 1), N_STREAM * HITS // HIT_DEV)
    assign_turns = jax.random.permutation(jax.random.fold_in(arg_keys[4], 3), N_STREAM * HITS // HIT_DEV)
    assign = jax.vmap(lambda own, number: routed_block(jax.random.fold_in(arg_keys[4], 2), own, number, HIT_DEV, N_STREAM, 1, CAP, 2))(assign_keys, assign_turns).reshape((N_STREAM, HITS, 1))
    token_in = bell_draw(arg_keys[5], (N_STREAM, TMIX, WT), WT ** -0.5, 1.25, ((0, 8),))
    token_out = bell_draw(arg_keys[6], (N_STREAM, WT, TMIX), TMIX ** -0.5, 0.3125, ((0, 8),))
    chan_in = bell_draw(arg_keys[7], (N_STREAM, C, HID), C ** -0.5, 0.5, ((0, 8),))
    chan_out = bell_draw(arg_keys[8], (N_STREAM, HID, C), HID ** -0.5, 0.25, ((0, 8),))
    readout = bell_draw(arg_keys[9], (N_MOD * C, C), (N_MOD * C) ** -0.5, 0.09375)
    latent_gain = jnp.clip(1.0 + 0.18 * jax.random.normal(arg_keys[10], (C,), jnp.float32), 0.1, 1.9)
    class_weight = bell_draw(arg_keys[11], (C, NCLS), C ** -0.5, 0.5, (), jnp.float32)
    return {"pixels": pixels, "stem_weight": stem_weight, "veto_weight": veto_weight, "hit_frames": hit_frames, "assign": assign, "token_in": token_in, "token_out": token_out, "chan_in": chan_in, "chan_out": chan_out, "readout": readout, "latent_gain": latent_gain, "class_weight": class_weight}


def rms_norm(values):
    return values * lax.rsqrt(lax.optimization_barrier(jnp.mean(values * values, axis=-1, keepdims=True)) + 1e-06)

def stem_layer(frame_pixels, stem_weight):
    count, height, width = frame_pixels.shape
    pixel_tiles = frame_pixels.astype(jnp.float32).reshape(count, height // PATCH, PATCH, width // PATCH, PATCH)
    kernel = stem_weight.astype(jnp.float32).reshape(PATCH, PATCH, -1)
    response = jnp.einsum('fapbq,pqc->fabc', pixel_tiles, kernel)
    return jax.nn.gelu(response).astype(jnp.bfloat16).reshape(count, -1, kernel.shape[-1])

def encode(tokens, mix_in, mix_out, chan_in, chan_out, readout, latent_gain, class_weight):
    batch = tokens.shape[0]
    channels = tokens.shape[-1]
    row_len = mix_in.shape[1]
    resid = tokens.astype(jnp.float32).reshape(batch, -1, row_len, channels)
    normed = rms_norm(resid).astype(jnp.bfloat16)
    mixed_tok = jax.nn.gelu(jnp.einsum('mw,brwc->brmc', mix_in.astype(jnp.float32), normed.astype(jnp.float32))).astype(jnp.bfloat16)
    after_mix = (resid + jnp.einsum('wm,brmc->brwc', mix_out.astype(jnp.float32), mixed_tok.astype(jnp.float32))).astype(jnp.bfloat16)
    mix_float = after_mix.astype(jnp.float32).reshape(batch, -1, channels)
    normed_two = rms_norm(mix_float).astype(jnp.bfloat16)
    hidden = jax.nn.gelu(jnp.einsum('btc,ch->bth', normed_two.astype(jnp.float32), chan_in.astype(jnp.float32))).astype(jnp.bfloat16)
    after_mlp = mix_float + jnp.einsum('bth,hc->btc', hidden.astype(jnp.float32), chan_out.astype(jnp.float32))
    pooled = lax.optimization_barrier(jnp.mean(after_mlp.reshape(batch, N_MOD, -1, channels), axis=2)).reshape(batch, -1).astype(jnp.bfloat16)
    projected = jnp.dot(pooled, readout, preferred_element_type=jnp.float32)
    latent = rms_norm(projected) * latent_gain
    class_scores = jnp.dot(latent, class_weight, precision=lax.Precision.HIGHEST)
    return (latent, class_scores)

def reference(pixels, stem_weight, veto_weight, hit_frames, assign, token_in, token_out, chan_in, chan_out, readout, latent_gain, class_weight):
    veto_rows = []
    latent_rows = []
    score_rows = []
    for stream_id in range(N_STREAM):
        features = stem_layer(pixels[stream_id], stem_weight)
        module_means = lax.optimization_barrier(jnp.mean(features.astype(jnp.float32).reshape(FRAMES, N_MOD, -1, C), axis=2))
        veto_rows.append(lax.optimization_barrier(jnp.sum(module_means * veto_weight, axis=(1, 2))))
        chosen = jnp.take(features, hit_frames[stream_id].astype(jnp.int32), axis=0)
        targets = assign[stream_id, :, 0].astype(jnp.int32)

        def encode_hit(payload):
            frame_tokens, target = payload
            latent, class_scores = encode(frame_tokens[None], token_in[target], token_out[target], chan_in[target], chan_out[target], readout, latent_gain, class_weight)
            return (latent[0], class_scores[0])
        hit_latents, hit_scores = lax.map(encode_hit, (chosen, targets))
        latent_rows.append(hit_latents)
        score_rows.append(hit_scores)
    return (jnp.stack(veto_rows), jnp.stack(latent_rows), jnp.stack(score_rows))
```

```python
import jax
import jax.numpy as jnp
from jax import lax
from jax.sharding import PartitionSpec as P

PATCH = 16


def rms_norm(values):
    return values * lax.rsqrt(jnp.mean(values * values, axis=-1, keepdims=True) + 1e-06)


def stem_layer(frame_pixels, stem_weight):
    count, height, width = frame_pixels.shape
    pixel_tiles = frame_pixels.reshape(count, height // PATCH, PATCH, width // PATCH, PATCH)
    kernel = stem_weight.reshape(PATCH, PATCH, -1)
    response = jnp.einsum(
        "fapbq,pqc->fabc", pixel_tiles, kernel, preferred_element_type=jnp.float32
    )
    return jax.nn.gelu(response).astype(jnp.bfloat16).reshape(count, -1, kernel.shape[-1])


def local(
    pixels,
    stem_weight,
    veto_weight,
    hit_frames,
    assign,
    token_in,
    token_out,
    chan_in,
    chan_out,
    readout,
    latent_gain,
    class_weight,
):
    f32 = jnp.float32
    bf16 = jnp.bfloat16
    stream_count = lax.axis_size("stream")
    mod_index = lax.axis_index("mod")

    pieces = (token_in[0], token_out[0], chan_in[0], chan_out[0])
    flat = jnp.concatenate([w.reshape(-1) for w in pieces])
    gathered = lax.all_gather(flat, "stream")
    weights, offset = [], 0
    for w in pieces:
        size = w.size
        weights.append(gathered[:, offset:offset + size].reshape((stream_count,) + w.shape))
        offset += size
    tin_all, tout_all, cin_all, cout_all = weights

    features = stem_layer(pixels[0], stem_weight)[:, :, :]
    channels = features.shape[-1]
    row_len = features.shape[1]

    means = jnp.mean(features.astype(f32), axis=1)
    row_weight = lax.dynamic_slice_in_dim(veto_weight, mod_index, 1, axis=0)
    veto_part = jnp.sum(means * row_weight, axis=1)
    veto = lax.psum_scatter(veto_part, "mod", scatter_dimension=0, tiled=True)

    hits = hit_frames[0]
    targets = assign[0, :, 0]
    order = jnp.argsort(targets, stable=True)
    sorted_targets = targets[order]
    x = jnp.take(features, hits[order], axis=0)
    resid = x.astype(f32)
    normed = rms_norm(resid).astype(bf16)
    tin_g = jnp.take(tin_all, sorted_targets, axis=0)
    tout_g = jnp.take(tout_all, sorted_targets, axis=0)
    mixed_tok = jax.nn.gelu(
        jnp.einsum("jmw,jwc->jmc", tin_g, normed, preferred_element_type=f32)
    ).astype(bf16)
    after_mix = (
        resid + jnp.einsum("jwm,jmc->jwc", tout_g, mixed_tok, preferred_element_type=f32)
    ).astype(bf16)
    hit_count = after_mix.shape[0]
    tokens = after_mix.reshape(hit_count * row_len, channels)
    group_sizes = (
        jnp.sum(targets[None, :] == jnp.arange(stream_count, dtype=targets.dtype)[:, None], axis=1)
        * row_len
    ).astype(jnp.int32)
    normed_two = rms_norm(tokens.astype(f32)).astype(bf16)
    hidden = jax.nn.gelu(
        lax.ragged_dot(normed_two, cin_all, group_sizes, preferred_element_type=f32)
    ).astype(bf16)
    after_mlp = tokens.astype(f32) + lax.ragged_dot(
        hidden, cout_all, group_sizes, preferred_element_type=f32
    )
    pooled_sorted = jnp.mean(after_mlp.reshape(hit_count, row_len, channels), axis=1).astype(bf16)
    pooled = jnp.zeros_like(pooled_sorted).at[order].set(pooled_sorted)
    row_readout = lax.dynamic_slice_in_dim(readout, mod_index * channels, channels, axis=0)
    projected_part = jnp.dot(pooled, row_readout, preferred_element_type=f32)
    projected = lax.psum_scatter(projected_part, "mod", scatter_dimension=0, tiled=True)
    latent = rms_norm(projected) * latent_gain
    class_scores = jnp.dot(latent, class_weight, precision=lax.Precision.HIGHEST)
    return (veto[None], latent[None], class_scores[None])


def solution(mesh):
    in_specs = (
        P("stream", None, "mod", None),
        P(),
        P(),
        P("stream", None),
        P("stream", None, None),
        P("stream", None, None),
        P("stream", None, None),
        P("stream", None, None),
        P("stream", None, None),
        P(),
        P(),
        P(),
    )
    out_specs = (P("stream", "mod"), P("stream", "mod", None), P("stream", "mod", None))
    return jax.shard_map(local, mesh=mesh, in_specs=in_specs, out_specs=out_specs, check_vma=False)
```

```python
import jax
import jax.numpy as jnp
from jax import lax
from jax.sharding import PartitionSpec as P

PATCH = 16


def rms_norm(values):
    return values * lax.rsqrt(jnp.mean(values * values, axis=-1, keepdims=True) + 1e-06)


def stem_layer(frame_pixels, stem_weight):
    count, height, width = frame_pixels.shape
    pixel_tiles = frame_pixels.reshape(count, height // PATCH, PATCH, width // PATCH, PATCH)
    kernel = stem_weight.reshape(PATCH, PATCH, -1)
    response = jnp.einsum(
        "fapbq,pqc->fabc", pixel_tiles, kernel, preferred_element_type=jnp.float32
    )
    return jax.nn.gelu(response).astype(jnp.bfloat16).reshape(count, -1, kernel.shape[-1])


def local(
    pixels,
    stem_weight,
    veto_weight,
    hit_frames,
    assign,
    token_in,
    token_out,
    chan_in,
    chan_out,
    readout,
    latent_gain,
    class_weight,
):
    f32 = jnp.float32
    bf16 = jnp.bfloat16
    stream_count = lax.axis_size("stream")
    mod_index = lax.axis_index("mod")

    pieces = (token_in[0], token_out[0], chan_in[0], chan_out[0])
    flat = jnp.concatenate([w.reshape(-1) for w in pieces])
    gathered = lax.all_gather(flat, "stream")
    weights, offset = [], 0
    for w in pieces:
        size = w.size
        weights.append(gathered[:, offset:offset + size].reshape((stream_count,) + w.shape))
        offset += size
    tin_all, tout_all, cin_all, cout_all = weights

    features = stem_layer(pixels[0], stem_weight)[:, :, :]
    channels = features.shape[-1]
    row_len = features.shape[1]

    means = jnp.mean(features.astype(f32), axis=1)
    row_weight = lax.dynamic_slice_in_dim(veto_weight, mod_index, 1, axis=0)
    veto_part = jnp.sum(means * row_weight, axis=1)

    hits = hit_frames[0]
    targets = assign[0, :, 0]
    order = jnp.argsort(targets, stable=True)
    sorted_targets = targets[order]
    x = jnp.take(features, hits[order], axis=0)
    resid = x.astype(f32)
    normed = rms_norm(resid).astype(bf16)
    tin_g = jnp.take(tin_all, sorted_targets, axis=0)
    tout_g = jnp.take(tout_all, sorted_targets, axis=0)
    mixed_tok = jax.nn.gelu(
        jnp.einsum("jmw,jwc->jmc", tin_g, normed, preferred_element_type=f32)
    ).astype(bf16)
    after_mix = (
        resid + jnp.einsum("jwm,jmc->jwc", tout_g, mixed_tok, preferred_element_type=f32)
    ).astype(bf16)
    hit_count = after_mix.shape[0]
    tokens = after_mix.reshape(hit_count * row_len, channels)
    group_sizes = (
        jnp.sum(targets[None, :] == jnp.arange(stream_count, dtype=targets.dtype)[:, None], axis=1)
        * row_len
    ).astype(jnp.int32)
    normed_two = rms_norm(tokens.astype(f32)).astype(bf16)
    hidden = jax.nn.gelu(
        lax.ragged_dot(normed_two, cin_all, group_sizes, preferred_element_type=f32)
    ).astype(bf16)
    after_mlp = tokens.astype(f32) + lax.ragged_dot(
        hidden, cout_all, group_sizes, preferred_element_type=f32
    )
    pooled_sorted = jnp.mean(after_mlp.reshape(hit_count, row_len, channels), axis=1).astype(bf16)
    pooled = jnp.zeros_like(pooled_sorted).at[order].set(pooled_sorted)
    row_readout = lax.dynamic_slice_in_dim(readout, mod_index * channels, channels, axis=0)
    projected_part = jnp.dot(pooled, row_readout, preferred_element_type=f32)
    module_count = lax.axis_size("mod")
    packed = jnp.concatenate(
        [
            projected_part.reshape(module_count, -1),
            veto_part.reshape(module_count, -1),
        ],
        axis=1,
    )
    received = lax.all_to_all(packed, "mod", split_axis=0, concat_axis=0, tiled=True)
    totals = jnp.sum(received, axis=0)
    split = projected_part.size // module_count
    projected = totals[:split].reshape(-1, channels)
    veto = totals[split:]
    latent = rms_norm(projected) * latent_gain
    class_scores = jnp.dot(latent, class_weight, precision=lax.Precision.HIGHEST)
    return (veto[None], latent[None], class_scores[None])


def solution(mesh):
    in_specs = (
        P("stream", None, "mod", None),
        P(),
        P(),
        P("stream", None),
        P("stream", None, None),
        P("stream", None, None),
        P("stream", None, None),
        P("stream", None, None),
        P("stream", None, None),
        P(),
        P(),
        P(),
    )
    out_specs = (P("stream", "mod"), P("stream", "mod", None), P("stream", "mod", None))
    return jax.shard_map(local, mesh=mesh, in_specs=in_specs, out_specs=out_specs, check_vma=False)
```

```python
import functools

import jax
import jax.numpy as jnp
from jax import lax
from jax.experimental import pallas as pl
from jax.experimental.pallas import tpu as pltpu
from jax.sharding import PartitionSpec as P

PATCH = 16
BLOCK_HITS = 16


def rms_norm(values):
    return values * lax.rsqrt(jnp.mean(values * values, axis=-1, keepdims=True) + 1e-06)


def stem_layer(frame_pixels, stem_weight):
    count, height, width = frame_pixels.shape
    pixel_tiles = frame_pixels.reshape(count, height // PATCH, PATCH, width // PATCH, PATCH)
    kernel = stem_weight.reshape(PATCH, PATCH, -1)
    response = jnp.einsum(
        "fapbq,pqc->fabc", pixel_tiles, kernel, preferred_element_type=jnp.float32
    )
    return jax.nn.gelu(response).astype(jnp.bfloat16).reshape(count, -1, kernel.shape[-1])


def encoder_kernel(
    tgt_ref, gstart_ref, gend_ref,
    x_ref, tin_ref, tout_ref, cin_ref, cout_ref, ro_ref,
    o_ref, mix_scr, hid_scr, out_scr,
):
    f32, bf16 = jnp.float32, jnp.bfloat16
    block = pl.program_id(0)
    hits, row_len, channels = x_ref.shape
    groups = cin_ref.shape[0]
    base = block * hits
    for h in range(hits):
        t = tgt_ref[base + h]
        xh = x_ref[h].astype(f32)
        normed = rms_norm(xh).astype(bf16)
        pre = jnp.dot(tin_ref[t], normed, preferred_element_type=f32)
        mixed = jax.nn.gelu(pre).astype(bf16)
        mix = jnp.dot(tout_ref[t], mixed, preferred_element_type=f32)
        mix_scr[h * row_len:(h + 1) * row_len, :] = (xh + mix).astype(bf16).astype(f32)
    after_mix = mix_scr[...]
    normed_two = rms_norm(after_mix).astype(bf16)
    token = base * row_len + lax.broadcasted_iota(jnp.int32, (hits * row_len, 1), 0)
    first = tgt_ref[base]
    last = tgt_ref[base + hits - 1]
    for g in range(groups):
        @pl.when((g >= first) & (g <= last))
        def _():
            inside = (token >= gstart_ref[g]) & (token < gend_ref[g])
            part = jnp.dot(normed_two, cin_ref[g], preferred_element_type=f32)
            hid_scr[...] = jnp.where(inside, part, hid_scr[...])
    hidden = jax.nn.gelu(hid_scr[...]).astype(bf16)
    for g in range(groups):
        @pl.when((g >= first) & (g <= last))
        def _():
            inside = (token >= gstart_ref[g]) & (token < gend_ref[g])
            part = jnp.dot(hidden, cout_ref[g], preferred_element_type=f32)
            out_scr[...] = jnp.where(inside, part, out_scr[...])
    after_mlp = after_mix + out_scr[...]
    pooled = jnp.mean(after_mlp.reshape(hits, row_len, channels), axis=1).astype(bf16)
    o_ref[...] = jnp.dot(pooled, ro_ref[...], preferred_element_type=f32)


def encode_rows(x, sorted_targets, gstart, gend, tin_all, tout_all, cin_all, cout_all, row_readout):
    hit_count, row_len, channels = x.shape
    steps = hit_count // BLOCK_HITS
    full = lambda a: pl.BlockSpec(a.shape, lambda i, *_: (0,) * a.ndim)
    grid_spec = pltpu.PrefetchScalarGridSpec(
        num_scalar_prefetch=3,
        grid=(steps,),
        in_specs=[
            pl.BlockSpec((BLOCK_HITS, row_len, channels), lambda i, *_: (i, 0, 0)),
            full(tin_all),
            full(tout_all),
            full(cin_all),
            full(cout_all),
            full(row_readout),
        ],
        out_specs=pl.BlockSpec((BLOCK_HITS, channels), lambda i, *_: (i, 0)),
        scratch_shapes=[
            pltpu.VMEM((BLOCK_HITS * row_len, channels), jnp.float32),
            pltpu.VMEM((BLOCK_HITS * row_len, cin_all.shape[-1]), jnp.float32),
            pltpu.VMEM((BLOCK_HITS * row_len, channels), jnp.float32),
        ],
    )
    return pl.pallas_call(
        encoder_kernel,
        grid_spec=grid_spec,
        out_shape=jax.ShapeDtypeStruct((hit_count, channels), jnp.float32),
        compiler_params=pltpu.CompilerParams(dimension_semantics=("arbitrary",)),
    )(sorted_targets, gstart, gend, x, tin_all, tout_all, cin_all, cout_all, row_readout)


def local(
    pixels,
    stem_weight,
    veto_weight,
    hit_frames,
    assign,
    token_in,
    token_out,
    chan_in,
    chan_out,
    readout,
    latent_gain,
    class_weight,
):
    f32 = jnp.float32
    stream_count = lax.axis_size("stream")
    module_count = lax.axis_size("mod")
    mod_index = lax.axis_index("mod")

    tin_all = lax.all_gather(token_in[0], "stream")
    tout_all = lax.all_gather(token_out[0], "stream")
    cin_all = lax.all_gather(chan_in[0], "stream")
    cout_all = lax.all_gather(chan_out[0], "stream")

    features = stem_layer(pixels[0], stem_weight)
    channels = features.shape[-1]
    row_len = features.shape[1]

    means = jnp.mean(features.astype(f32), axis=1)
    row_weight = lax.dynamic_slice_in_dim(veto_weight, mod_index, 1, axis=0)
    veto_part = jnp.sum(means * row_weight, axis=1)

    hits = hit_frames[0]
    targets = assign[0, :, 0].astype(jnp.int32)
    order = jnp.argsort(targets, stable=True)
    sorted_targets = targets[order]
    x = jnp.take(features, hits[order], axis=0)
    counts = jnp.sum(
        (targets[None, :] == jnp.arange(stream_count, dtype=jnp.int32)[:, None]).astype(jnp.int32),
        axis=1,
    )
    gend = jnp.cumsum(counts) * row_len
    gstart = gend - counts * row_len
    row_readout = lax.dynamic_slice_in_dim(readout, mod_index * channels, channels, axis=0)
    projected_sorted = encode_rows(
        x, sorted_targets, gstart.astype(jnp.int32), gend.astype(jnp.int32),
        tin_all, tout_all, cin_all, cout_all, row_readout,
    )
    projected_part = jnp.zeros_like(projected_sorted).at[order].set(projected_sorted)

    packed = jnp.concatenate(
        [
            projected_part.reshape(module_count, -1),
            veto_part.reshape(module_count, -1),
        ],
        axis=1,
    )
    received = lax.all_to_all(packed, "mod", split_axis=0, concat_axis=0, tiled=True)
    totals = jnp.sum(received, axis=0)
    split = projected_part.size // module_count
    projected = totals[:split].reshape(-1, channels)
    veto = totals[split:]
    latent = rms_norm(projected) * latent_gain
    class_scores = jnp.dot(latent, class_weight, precision=lax.Precision.HIGHEST)
    return (veto[None], latent[None], class_scores[None])


def solution(mesh):
    in_specs = (
        P("stream", None, "mod", None),
        P(),
        P(),
        P("stream", None),
        P("stream", None, None),
        P("stream", None, None),
        P("stream", None, None),
        P("stream", None, None),
        P("stream", None, None),
        P(),
        P(),
        P(),
    )
    out_specs = (P("stream", "mod"), P("stream", "mod", None), P("stream", "mod", None))
    return jax.shard_map(local, mesh=mesh, in_specs=in_specs, out_specs=out_specs, check_vma=False)
```

```python
import functools

import jax
import jax.numpy as jnp
from jax import lax
from jax.experimental import pallas as pl
from jax.experimental.pallas import tpu as pltpu
from jax.sharding import PartitionSpec as P

PATCH = 16
BLOCK_HITS = 16


def rms_norm(values):
    return values * lax.rsqrt(jnp.mean(values * values, axis=-1, keepdims=True) + 1e-06)


def stem_layer(frame_pixels, stem_weight):
    count, height, width = frame_pixels.shape
    pixel_tiles = frame_pixels.reshape(count, height // PATCH, PATCH, width // PATCH, PATCH)
    kernel = stem_weight.reshape(PATCH, PATCH, -1)
    response = jnp.einsum(
        "fapbq,pqc->fabc", pixel_tiles, kernel, preferred_element_type=jnp.float32
    )
    return jax.nn.gelu(response).astype(jnp.bfloat16).reshape(count, -1, kernel.shape[-1])


def encoder_kernel(
    tgt_ref, gstart_ref, gend_ref,
    x_ref, tin_ref, tout_ref, cin_ref, cout_ref, ro_ref,
    o_ref, mix_scr, hid_scr, out_scr,
):
    f32, bf16 = jnp.float32, jnp.bfloat16
    block = pl.program_id(0)
    hits, row_len, channels = x_ref.shape
    groups = cin_ref.shape[0]
    base = block * hits
    for h in range(hits):
        t = tgt_ref[base + h]
        xh = x_ref[h].astype(f32)
        normed = rms_norm(xh).astype(bf16)
        pre = jnp.dot(tin_ref[t], normed, preferred_element_type=f32)
        mixed = jax.nn.gelu(pre).astype(bf16)
        mix = jnp.dot(tout_ref[t], mixed, preferred_element_type=f32)
        mix_scr[h * row_len:(h + 1) * row_len, :] = (xh + mix).astype(bf16).astype(f32)
    after_mix = mix_scr[...]
    normed_two = rms_norm(after_mix).astype(bf16)
    token = base * row_len + lax.broadcasted_iota(jnp.int32, (hits * row_len, 1), 0)
    first = tgt_ref[base]
    last = tgt_ref[base + hits - 1]
    for g in range(groups):
        @pl.when((g >= first) & (g <= last))
        def _():
            inside = (token >= gstart_ref[g]) & (token < gend_ref[g])
            part = jnp.dot(normed_two, cin_ref[g], preferred_element_type=f32)
            hid_scr[...] = jnp.where(inside, part, hid_scr[...])
    hidden = jax.nn.gelu(hid_scr[...]).astype(bf16)
    for g in range(groups):
        @pl.when((g >= first) & (g <= last))
        def _():
            inside = (token >= gstart_ref[g]) & (token < gend_ref[g])
            part = jnp.dot(hidden, cout_ref[g], preferred_element_type=f32)
            out_scr[...] = jnp.where(inside, part, out_scr[...])
    after_mlp = after_mix + out_scr[...]
    pooled = jnp.mean(after_mlp.reshape(hits, row_len, channels), axis=1).astype(bf16)
    o_ref[...] = jnp.dot(pooled, ro_ref[...], preferred_element_type=f32)


def encode_rows(x, sorted_targets, gstart, gend, tin_all, tout_all, cin_all, cout_all, row_readout):
    hit_count, row_len, channels = x.shape
    steps = hit_count // BLOCK_HITS
    full = lambda a: pl.BlockSpec(a.shape, lambda i, *_: (0,) * a.ndim)
    grid_spec = pltpu.PrefetchScalarGridSpec(
        num_scalar_prefetch=3,
        grid=(steps,),
        in_specs=[
            pl.BlockSpec((BLOCK_HITS, row_len, channels), lambda i, *_: (i, 0, 0)),
            full(tin_all),
            full(tout_all),
            full(cin_all),
            full(cout_all),
            full(row_readout),
        ],
        out_specs=pl.BlockSpec((BLOCK_HITS, channels), lambda i, *_: (i, 0)),
        scratch_shapes=[
            pltpu.VMEM((BLOCK_HITS * row_len, channels), jnp.float32),
            pltpu.VMEM((BLOCK_HITS * row_len, cin_all.shape[-1]), jnp.float32),
            pltpu.VMEM((BLOCK_HITS * row_len, channels), jnp.float32),
        ],
    )
    return pl.pallas_call(
        encoder_kernel,
        grid_spec=grid_spec,
        out_shape=jax.ShapeDtypeStruct((hit_count, channels), jnp.float32),
        compiler_params=pltpu.CompilerParams(dimension_semantics=("arbitrary",)),
    )(sorted_targets, gstart, gend, x, tin_all, tout_all, cin_all, cout_all, row_readout)


def local(
    pixels,
    stem_weight,
    veto_weight,
    hit_frames,
    assign,
    token_in,
    token_out,
    chan_in,
    chan_out,
    readout,
    latent_gain,
    class_weight,
):
    f32 = jnp.float32
    stream_count = lax.axis_size("stream")
    module_count = lax.axis_size("mod")
    mod_index = lax.axis_index("mod")

    pieces = (token_in[0], token_out[0], chan_in[0], chan_out[0])
    gathered = lax.all_gather(jnp.concatenate([w.reshape(-1) for w in pieces]), "stream")
    weights, offset = [], 0
    for w in pieces:
        weights.append(gathered[:, offset:offset + w.size].reshape((stream_count,) + w.shape))
        offset += w.size
    tin_all, tout_all, cin_all, cout_all = weights

    features = stem_layer(pixels[0], stem_weight)
    channels = features.shape[-1]
    row_len = features.shape[1]

    means = jnp.mean(features.astype(f32), axis=1)
    row_weight = lax.dynamic_slice_in_dim(veto_weight, mod_index, 1, axis=0)
    veto_part = jnp.sum(means * row_weight, axis=1)

    hits = hit_frames[0]
    targets = assign[0, :, 0].astype(jnp.int32)
    order = jnp.argsort(targets, stable=True)
    sorted_targets = targets[order]
    x = jnp.take(features, hits[order], axis=0)
    counts = jnp.sum(
        (targets[None, :] == jnp.arange(stream_count, dtype=jnp.int32)[:, None]).astype(jnp.int32),
        axis=1,
    )
    gend = jnp.cumsum(counts) * row_len
    gstart = gend - counts * row_len
    row_readout = lax.dynamic_slice_in_dim(readout, mod_index * channels, channels, axis=0)
    projected_sorted = encode_rows(
        x, sorted_targets, gstart.astype(jnp.int32), gend.astype(jnp.int32),
        tin_all, tout_all, cin_all, cout_all, row_readout,
    )
    projected_part = jnp.zeros_like(projected_sorted).at[order].set(projected_sorted)

    packed = jnp.concatenate(
        [
            projected_part.reshape(module_count, -1),
            veto_part.reshape(module_count, -1),
        ],
        axis=1,
    )
    received = lax.all_to_all(packed, "mod", split_axis=0, concat_axis=0, tiled=True)
    totals = jnp.sum(received, axis=0)
    split = projected_part.size // module_count
    projected = totals[:split].reshape(-1, channels)
    veto = totals[split:]
    latent = rms_norm(projected) * latent_gain
    class_scores = jnp.dot(latent, class_weight, precision=lax.Precision.HIGHEST)
    return (veto[None], latent[None], class_scores[None])


def solution(mesh):
    in_specs = (
        P("stream", None, "mod", None),
        P(),
        P(),
        P("stream", None),
        P("stream", None, None),
        P("stream", None, None),
        P("stream", None, None),
        P("stream", None, None),
        P("stream", None, None),
        P(),
        P(),
        P(),
    )
    out_specs = (P("stream", "mod"), P("stream", "mod", None), P("stream", "mod", None))
    return jax.shard_map(local, mesh=mesh, in_specs=in_specs, out_specs=out_specs, check_vma=False)
```

```python
import functools

import jax
import jax.numpy as jnp
from jax import lax
from jax.experimental import pallas as pl
from jax.experimental.pallas import tpu as pltpu
from jax.sharding import PartitionSpec as P

PATCH = 16
BLOCK_HITS = 16


def rms_norm(values):
    return values * lax.rsqrt(jnp.mean(values * values, axis=-1, keepdims=True) + 1e-06)


def stem_layer(frame_pixels, stem_weight):
    count, height, width = frame_pixels.shape
    pixel_tiles = frame_pixels.reshape(count, height // PATCH, PATCH, width // PATCH, PATCH)
    kernel = stem_weight.reshape(PATCH, PATCH, -1)
    response = jnp.einsum(
        "fapbq,pqc->fabc", pixel_tiles, kernel, preferred_element_type=jnp.float32
    )
    return jax.nn.gelu(response).astype(jnp.bfloat16).reshape(count, -1, kernel.shape[-1])


def encoder_kernel(
    tgt_ref, gstart_ref, gend_ref,
    x_ref, tin_ref, tout_ref, cin_ref, cout_ref, ro_ref,
    o_ref, mix_scr, hid_scr, out_scr,
):
    f32, bf16 = jnp.float32, jnp.bfloat16
    block = pl.program_id(0)
    hits, row_len, channels = x_ref.shape
    groups = cin_ref.shape[0]
    base = block * hits
    for h in range(hits):
        t = tgt_ref[base + h]
        xh = x_ref[h].astype(f32)
        normed = rms_norm(xh).astype(bf16)
        pre = jnp.dot(tin_ref[t], normed, preferred_element_type=f32)
        mixed = jax.nn.gelu(pre).astype(bf16)
        mix = jnp.dot(tout_ref[t], mixed, preferred_element_type=f32)
        mix_scr[h * row_len:(h + 1) * row_len, :] = (xh + mix).astype(bf16).astype(f32)
    after_mix = mix_scr[...]
    normed_two = rms_norm(after_mix).astype(bf16)
    token = base * row_len + lax.broadcasted_iota(jnp.int32, (hits * row_len, 1), 0)
    first = tgt_ref[base]
    last = tgt_ref[base + hits - 1]
    for g in range(groups):
        @pl.when((g >= first) & (g <= last))
        def _():
            inside = (token >= gstart_ref[g]) & (token < gend_ref[g])
            part = jnp.dot(normed_two, cin_ref[g], preferred_element_type=f32)
            hid_scr[...] = jnp.where(inside, part, hid_scr[...])
    hidden = jax.nn.gelu(hid_scr[...]).astype(bf16)
    for g in range(groups):
        @pl.when((g >= first) & (g <= last))
        def _():
            inside = (token >= gstart_ref[g]) & (token < gend_ref[g])
            part = jnp.dot(hidden, cout_ref[g], preferred_element_type=f32)
            out_scr[...] = jnp.where(inside, part, out_scr[...])
    after_mlp = after_mix + out_scr[...]
    pooled = jnp.mean(after_mlp.reshape(hits, row_len, channels), axis=1).astype(bf16)
    o_ref[...] = jnp.dot(pooled, ro_ref[...], preferred_element_type=f32)


def encode_rows(x, sorted_targets, gstart, gend, tin_all, tout_all, cin_all, cout_all, row_readout):
    hit_count, row_len, channels = x.shape
    steps = hit_count // BLOCK_HITS
    full = lambda a: pl.BlockSpec(a.shape, lambda i, *_: (0,) * a.ndim)
    grid_spec = pltpu.PrefetchScalarGridSpec(
        num_scalar_prefetch=3,
        grid=(steps,),
        in_specs=[
            pl.BlockSpec((BLOCK_HITS, row_len, channels), lambda i, *_: (i, 0, 0)),
            full(tin_all),
            full(tout_all),
            full(cin_all),
            full(cout_all),
            full(row_readout),
        ],
        out_specs=pl.BlockSpec((BLOCK_HITS, channels), lambda i, *_: (i, 0)),
        scratch_shapes=[
            pltpu.VMEM((BLOCK_HITS * row_len, channels), jnp.float32),
            pltpu.VMEM((BLOCK_HITS * row_len, cin_all.shape[-1]), jnp.float32),
            pltpu.VMEM((BLOCK_HITS * row_len, channels), jnp.float32),
        ],
    )
    return pl.pallas_call(
        encoder_kernel,
        grid_spec=grid_spec,
        out_shape=jax.ShapeDtypeStruct((hit_count, channels), jnp.float32),
        compiler_params=pltpu.CompilerParams(dimension_semantics=("arbitrary",)),
    )(sorted_targets, gstart, gend, x, tin_all, tout_all, cin_all, cout_all, row_readout)


def local(
    pixels,
    stem_weight,
    veto_weight,
    hit_frames,
    assign,
    token_in,
    token_out,
    chan_in,
    chan_out,
    readout,
    latent_gain,
    class_weight,
):
    f32 = jnp.float32
    stream_count = lax.axis_size("stream")
    module_count = lax.axis_size("mod")
    mod_index = lax.axis_index("mod")

    pieces = (token_in[0], token_out[0])
    gathered = lax.all_gather(jnp.concatenate([w.reshape(-1) for w in pieces]), "stream")
    weights, offset = [], 0
    for w in pieces:
        weights.append(gathered[:, offset:offset + w.size].reshape((stream_count,) + w.shape))
        offset += w.size
    tin_all, tout_all = weights
    cin_all = lax.all_gather(chan_in[0], "stream")
    cout_all = lax.all_gather(chan_out[0], "stream")

    features = stem_layer(pixels[0], stem_weight)
    channels = features.shape[-1]
    row_len = features.shape[1]

    means = jnp.mean(features.astype(f32), axis=1)
    row_weight = lax.dynamic_slice_in_dim(veto_weight, mod_index, 1, axis=0)
    veto_part = jnp.sum(means * row_weight, axis=1)

    hits = hit_frames[0]
    targets = assign[0, :, 0].astype(jnp.int32)
    position = jnp.arange(targets.shape[0], dtype=jnp.int32)
    before = (targets[None, :] < targets[:, None]) | (
        (targets[None, :] == targets[:, None]) & (position[None, :] < position[:, None])
    )
    rank = jnp.sum(before.astype(jnp.int32), axis=1)
    picks = rank[None, :] == position[:, None]
    sorted_targets = jnp.sum(jnp.where(picks, targets[None, :], 0), axis=1)
    sorted_frames = jnp.sum(jnp.where(picks, hits[None, :], 0), axis=1)
    x = jnp.take(features, sorted_frames, axis=0)
    counts = jnp.sum(
        (targets[None, :] == jnp.arange(stream_count, dtype=jnp.int32)[:, None]).astype(jnp.int32),
        axis=1,
    )
    gend = jnp.cumsum(counts) * row_len
    gstart = gend - counts * row_len
    row_readout = lax.dynamic_slice_in_dim(readout, mod_index * channels, channels, axis=0)
    projected_sorted = encode_rows(
        x, sorted_targets, gstart.astype(jnp.int32), gend.astype(jnp.int32),
        tin_all, tout_all, cin_all, cout_all, row_readout,
    )
    projected_part = jnp.take(projected_sorted, rank, axis=0)

    packed = jnp.concatenate(
        [
            projected_part.reshape(module_count, -1),
            veto_part.reshape(module_count, -1),
        ],
        axis=1,
    )
    received = lax.all_to_all(packed, "mod", split_axis=0, concat_axis=0, tiled=True)
    totals = jnp.sum(received, axis=0)
    split = projected_part.size // module_count
    projected = totals[:split].reshape(-1, channels)
    veto = totals[split:]
    latent = rms_norm(projected) * latent_gain
    class_scores = jnp.dot(latent, class_weight, precision=lax.Precision.HIGHEST)
    return (veto[None], latent[None], class_scores[None])


def solution(mesh):
    in_specs = (
        P("stream", None, "mod", None),
        P(),
        P(),
        P("stream", None),
        P("stream", None, None),
        P("stream", None, None),
        P("stream", None, None),
        P("stream", None, None),
        P("stream", None, None),
        P(),
        P(),
        P(),
    )
    out_specs = (P("stream", "mod"), P("stream", "mod", None), P("stream", "mod", None))
    return jax.shard_map(local, mesh=mesh, in_specs=in_specs, out_specs=out_specs, check_vma=False)
```

```python
import functools

import jax
import jax.numpy as jnp
from jax import lax
from jax.experimental import pallas as pl
from jax.experimental.pallas import tpu as pltpu
from jax.sharding import PartitionSpec as P

PATCH = 16
BLOCK_HITS = 16


def rms_norm(values):
    return values * lax.rsqrt(jnp.mean(values * values, axis=-1, keepdims=True) + 1e-06)


def stem_layer(frame_pixels, stem_weight):
    count, height, width = frame_pixels.shape
    pixel_tiles = frame_pixels.reshape(count, height // PATCH, PATCH, width // PATCH, PATCH)
    kernel = stem_weight.reshape(PATCH, PATCH, -1)
    response = jnp.einsum(
        "fapbq,pqc->fabc", pixel_tiles, kernel, preferred_element_type=jnp.float32
    )
    return jax.nn.gelu(response).astype(jnp.bfloat16).reshape(count, -1, kernel.shape[-1])


def encoder_kernel(
    tgt_ref, gstart_ref, gend_ref,
    x_ref, tin_ref, tout_ref, cin_ref, cout_ref, ro_ref,
    o_ref, mix_scr, hid_scr, out_scr,
):
    f32, bf16 = jnp.float32, jnp.bfloat16
    block = pl.program_id(0)
    hits, row_len, channels = x_ref.shape
    groups = cin_ref.shape[0]
    base = block * hits
    for h in range(hits):
        t = tgt_ref[base + h]
        xh = x_ref[h].astype(f32)
        normed = rms_norm(xh).astype(bf16)
        pre = jnp.dot(tin_ref[t], normed, preferred_element_type=f32)
        mixed = jax.nn.gelu(pre).astype(bf16)
        mix = jnp.dot(tout_ref[t], mixed, preferred_element_type=f32)
        mix_scr[h * row_len:(h + 1) * row_len, :] = (xh + mix).astype(bf16).astype(f32)
    after_mix = mix_scr[...]
    normed_two = rms_norm(after_mix).astype(bf16)
    token = base * row_len + lax.broadcasted_iota(jnp.int32, (hits * row_len, 1), 0)
    first = tgt_ref[base]
    last = tgt_ref[base + hits - 1]
    for g in range(groups):
        @pl.when((g >= first) & (g <= last))
        def _():
            inside = (token >= gstart_ref[g]) & (token < gend_ref[g])
            part = jnp.dot(normed_two, cin_ref[g], preferred_element_type=f32)
            hid_scr[...] = jnp.where(inside, part, hid_scr[...])
    hidden = jax.nn.gelu(hid_scr[...]).astype(bf16)
    for g in range(groups):
        @pl.when((g >= first) & (g <= last))
        def _():
            inside = (token >= gstart_ref[g]) & (token < gend_ref[g])
            part = jnp.dot(hidden, cout_ref[g], preferred_element_type=f32)
            out_scr[...] = jnp.where(inside, part, out_scr[...])
    after_mlp = after_mix + out_scr[...]
    pooled = jnp.mean(after_mlp.reshape(hits, row_len, channels), axis=1).astype(bf16)
    o_ref[...] = jnp.dot(pooled, ro_ref[...], preferred_element_type=f32)


def encode_rows(x, sorted_targets, gstart, gend, tin_all, tout_all, cin_all, cout_all, row_readout):
    hit_count, row_len, channels = x.shape
    steps = hit_count // BLOCK_HITS
    full = lambda a: pl.BlockSpec(a.shape, lambda i, *_: (0,) * a.ndim)
    grid_spec = pltpu.PrefetchScalarGridSpec(
        num_scalar_prefetch=3,
        grid=(steps,),
        in_specs=[
            pl.BlockSpec((BLOCK_HITS, row_len, channels), lambda i, *_: (i, 0, 0)),
            full(tin_all),
            full(tout_all),
            full(cin_all),
            full(cout_all),
            full(row_readout),
        ],
        out_specs=pl.BlockSpec((BLOCK_HITS, channels), lambda i, *_: (i, 0)),
        scratch_shapes=[
            pltpu.VMEM((BLOCK_HITS * row_len, channels), jnp.float32),
            pltpu.VMEM((BLOCK_HITS * row_len, cin_all.shape[-1]), jnp.float32),
            pltpu.VMEM((BLOCK_HITS * row_len, channels), jnp.float32),
        ],
    )
    return pl.pallas_call(
        encoder_kernel,
        grid_spec=grid_spec,
        out_shape=jax.ShapeDtypeStruct((hit_count, channels), jnp.float32),
        compiler_params=pltpu.CompilerParams(dimension_semantics=("arbitrary",)),
    )(sorted_targets, gstart, gend, x, tin_all, tout_all, cin_all, cout_all, row_readout)


def local(
    pixels,
    stem_weight,
    veto_weight,
    hit_frames,
    assign,
    token_in,
    token_out,
    chan_in,
    chan_out,
    readout,
    latent_gain,
    class_weight,
):
    f32 = jnp.float32
    stream_count = lax.axis_size("stream")
    module_count = lax.axis_size("mod")
    mod_index = lax.axis_index("mod")

    pieces = (token_in[0], token_out[0], chan_in[0], chan_out[0])
    gathered = lax.all_gather(jnp.concatenate([w.reshape(-1) for w in pieces]), "stream")
    weights, offset = [], 0
    for w in pieces:
        weights.append(gathered[:, offset:offset + w.size].reshape((stream_count,) + w.shape))
        offset += w.size
    tin_all, tout_all, cin_all, cout_all = weights

    features = stem_layer(pixels[0], stem_weight)
    channels = features.shape[-1]
    row_len = features.shape[1]

    means = jnp.mean(features.astype(f32), axis=1)
    row_weight = lax.dynamic_slice_in_dim(veto_weight, mod_index, 1, axis=0)
    veto_part = jnp.sum(means * row_weight, axis=1)

    hits = hit_frames[0]
    targets = assign[0, :, 0].astype(jnp.int32)
    position = jnp.arange(targets.shape[0], dtype=jnp.int32)
    before = (targets[None, :] < targets[:, None]) | (
        (targets[None, :] == targets[:, None]) & (position[None, :] < position[:, None])
    )
    rank = jnp.sum(before.astype(jnp.int32), axis=1)
    picks = rank[None, :] == position[:, None]
    sorted_targets = jnp.sum(jnp.where(picks, targets[None, :], 0), axis=1)
    sorted_frames = jnp.sum(jnp.where(picks, hits[None, :], 0), axis=1)
    x = jnp.take(features, sorted_frames, axis=0)
    counts = jnp.sum(
        (targets[None, :] == jnp.arange(stream_count, dtype=jnp.int32)[:, None]).astype(jnp.int32),
        axis=1,
    )
    gend = jnp.cumsum(counts) * row_len
    gstart = gend - counts * row_len
    row_readout = lax.dynamic_slice_in_dim(readout, mod_index * channels, channels, axis=0)
    projected_sorted = encode_rows(
        x, sorted_targets, gstart.astype(jnp.int32), gend.astype(jnp.int32),
        tin_all, tout_all, cin_all, cout_all, row_readout,
    )
    projected_part = jnp.take(projected_sorted, rank, axis=0)

    packed = jnp.concatenate(
        [
            projected_part.reshape(module_count, -1),
            veto_part.reshape(module_count, -1),
        ],
        axis=1,
    )
    received = lax.all_to_all(packed, "mod", split_axis=0, concat_axis=0, tiled=True)
    totals = jnp.sum(received, axis=0)
    split = projected_part.size // module_count
    projected = totals[:split].reshape(-1, channels)
    veto = totals[split:]
    latent = rms_norm(projected) * latent_gain
    class_scores = jnp.dot(latent, class_weight, precision=lax.Precision.HIGHEST)
    return (veto[None], latent[None], class_scores[None])


def solution(mesh):
    in_specs = (
        P("stream", None, "mod", None),
        P(),
        P(),
        P("stream", None),
        P("stream", None, None),
        P("stream", None, None),
        P("stream", None, None),
        P("stream", None, None),
        P("stream", None, None),
        P(),
        P(),
        P(),
    )
    out_specs = (P("stream", "mod"), P("stream", "mod", None), P("stream", "mod", None))
    return jax.shard_map(local, mesh=mesh, in_specs=in_specs, out_specs=out_specs, check_vma=False)
```

```python
import functools

import jax
import jax.numpy as jnp
from jax import lax
from jax.experimental import pallas as pl
from jax.experimental.pallas import tpu as pltpu
from jax.sharding import PartitionSpec as P

PATCH = 16
BLOCK_HITS = 16


def rms_norm(values):
    return values * lax.rsqrt(jnp.mean(values * values, axis=-1, keepdims=True) + 1e-06)


def stem_layer(frame_pixels, stem_weight):
    count, height, width = frame_pixels.shape
    pixel_tiles = frame_pixels.reshape(count, height // PATCH, PATCH, width // PATCH, PATCH)
    kernel = stem_weight.reshape(PATCH, PATCH, -1)
    response = jnp.einsum(
        "fapbq,pqc->fabc", pixel_tiles, kernel, preferred_element_type=jnp.float32
    )
    return jax.nn.gelu(response).astype(jnp.bfloat16).reshape(count, -1, kernel.shape[-1])


def encoder_kernel(
    tgt_ref, gstart_ref, gend_ref,
    x_ref, tin_ref, tout_ref, cin_ref, cout_ref, ro_ref,
    o_ref, mix_scr, hid_scr, out_scr,
):
    f32, bf16 = jnp.float32, jnp.bfloat16
    block = pl.program_id(0)
    hits, row_len, channels = x_ref.shape
    groups = cin_ref.shape[0]
    base = block * hits
    for h in range(hits):
        t = tgt_ref[base + h]
        xh = x_ref[h].astype(f32)
        normed = rms_norm(xh).astype(bf16)
        pre = jnp.dot(tin_ref[t], normed, preferred_element_type=f32)
        mixed = jax.nn.gelu(pre).astype(bf16)
        mix = jnp.dot(tout_ref[t], mixed, preferred_element_type=f32)
        mix_scr[h * row_len:(h + 1) * row_len, :] = (xh + mix).astype(bf16).astype(f32)
    after_mix = mix_scr[...]
    normed_two = rms_norm(after_mix).astype(bf16)
    token = base * row_len + lax.broadcasted_iota(jnp.int32, (hits * row_len, 1), 0)
    first = tgt_ref[base]
    last = tgt_ref[base + hits - 1]
    for g in range(groups):
        @pl.when((g >= first) & (g <= last))
        def _():
            inside = (token >= gstart_ref[g]) & (token < gend_ref[g])
            part = jnp.dot(normed_two, cin_ref[g], preferred_element_type=f32)
            hid_scr[...] = jnp.where(inside, part, hid_scr[...])
    hidden = jax.nn.gelu(hid_scr[...]).astype(bf16)
    for g in range(groups):
        @pl.when((g >= first) & (g <= last))
        def _():
            inside = (token >= gstart_ref[g]) & (token < gend_ref[g])
            part = jnp.dot(hidden, cout_ref[g], preferred_element_type=f32)
            out_scr[...] = jnp.where(inside, part, out_scr[...])
    after_mlp = after_mix + out_scr[...]
    pooled = jnp.mean(after_mlp.reshape(hits, row_len, channels), axis=1).astype(bf16)
    o_ref[...] = jnp.dot(pooled, ro_ref[...], preferred_element_type=f32)


def encode_rows(x, sorted_targets, gstart, gend, tin_all, tout_all, cin_all, cout_all, row_readout):
    hit_count, row_len, channels = x.shape
    steps = hit_count // BLOCK_HITS
    full = lambda a: pl.BlockSpec(a.shape, lambda i, *_: (0,) * a.ndim)
    grid_spec = pltpu.PrefetchScalarGridSpec(
        num_scalar_prefetch=3,
        grid=(steps,),
        in_specs=[
            pl.BlockSpec((BLOCK_HITS, row_len, channels), lambda i, *_: (i, 0, 0)),
            full(tin_all),
            full(tout_all),
            full(cin_all),
            full(cout_all),
            full(row_readout),
        ],
        out_specs=pl.BlockSpec((BLOCK_HITS, channels), lambda i, *_: (i, 0)),
        scratch_shapes=[
            pltpu.VMEM((BLOCK_HITS * row_len, channels), jnp.float32),
            pltpu.VMEM((BLOCK_HITS * row_len, cin_all.shape[-1]), jnp.float32),
            pltpu.VMEM((BLOCK_HITS * row_len, channels), jnp.float32),
        ],
    )
    return pl.pallas_call(
        encoder_kernel,
        grid_spec=grid_spec,
        out_shape=jax.ShapeDtypeStruct((hit_count, channels), jnp.float32),
        compiler_params=pltpu.CompilerParams(dimension_semantics=("arbitrary",)),
    )(sorted_targets, gstart, gend, x, tin_all, tout_all, cin_all, cout_all, row_readout)


def exchange_kernel(n, x_ref, o_ref, recv, send_sems, recv_sems):
    me = lax.axis_index("mod")
    stream = lax.axis_index("stream")
    barrier = pltpu.get_barrier_semaphore()
    for d in range(1, n):
        pl.semaphore_signal(
            barrier, inc=1, device_id=(stream, lax.rem(me + d, n)),
            device_id_type=pl.DeviceIdType.MESH,
        )
    pl.semaphore_wait(barrier, n - 1)
    copies = []
    for d in range(1, n):
        target = lax.rem(me + d, n)
        copy = pltpu.make_async_remote_copy(
            src_ref=x_ref.at[target],
            dst_ref=recv.at[d - 1],
            send_sem=send_sems.at[d - 1],
            recv_sem=recv_sems.at[d - 1],
            device_id=(stream, target),
            device_id_type=pl.DeviceIdType.MESH,
        )
        copy.start()
        copies.append(copy)
    for copy in copies:
        copy.wait()
    total = x_ref[me]
    for d in range(n - 1):
        total = total + recv[d]
    o_ref[...] = total


def exchange_sum(x):
    n = x.shape[0]
    return pl.pallas_call(
        functools.partial(exchange_kernel, n),
        out_shape=jax.ShapeDtypeStruct(x.shape[1:], x.dtype),
        in_specs=[pl.BlockSpec(memory_space=pltpu.VMEM)],
        out_specs=pl.BlockSpec(memory_space=pltpu.VMEM),
        scratch_shapes=[
            pltpu.VMEM((n - 1,) + x.shape[1:], x.dtype),
            pltpu.SemaphoreType.DMA((n - 1,)),
            pltpu.SemaphoreType.DMA((n - 1,)),
        ],
        compiler_params=pltpu.CompilerParams(collective_id=0, has_side_effects=True),
    )(x)


def local(
    pixels,
    stem_weight,
    veto_weight,
    hit_frames,
    assign,
    token_in,
    token_out,
    chan_in,
    chan_out,
    readout,
    latent_gain,
    class_weight,
):
    f32 = jnp.float32
    stream_count = lax.axis_size("stream")
    module_count = lax.axis_size("mod")
    mod_index = lax.axis_index("mod")

    pieces = (token_in[0], token_out[0], chan_in[0], chan_out[0])
    gathered = lax.all_gather(jnp.concatenate([w.reshape(-1) for w in pieces]), "stream")
    weights, offset = [], 0
    for w in pieces:
        weights.append(gathered[:, offset:offset + w.size].reshape((stream_count,) + w.shape))
        offset += w.size
    tin_all, tout_all, cin_all, cout_all = weights

    features = stem_layer(pixels[0], stem_weight)
    channels = features.shape[-1]
    row_len = features.shape[1]

    means = jnp.mean(features.astype(f32), axis=1)
    row_weight = lax.dynamic_slice_in_dim(veto_weight, mod_index, 1, axis=0)
    veto_part = jnp.sum(means * row_weight, axis=1)

    hits = hit_frames[0]
    targets = assign[0, :, 0].astype(jnp.int32)
    position = jnp.arange(targets.shape[0], dtype=jnp.int32)
    before = (targets[None, :] < targets[:, None]) | (
        (targets[None, :] == targets[:, None]) & (position[None, :] < position[:, None])
    )
    rank = jnp.sum(before.astype(jnp.int32), axis=1)
    picks = rank[None, :] == position[:, None]
    sorted_targets = jnp.sum(jnp.where(picks, targets[None, :], 0), axis=1)
    sorted_frames = jnp.sum(jnp.where(picks, hits[None, :], 0), axis=1)
    x = jnp.take(features, sorted_frames, axis=0)
    counts = jnp.sum(
        (targets[None, :] == jnp.arange(stream_count, dtype=jnp.int32)[:, None]).astype(jnp.int32),
        axis=1,
    )
    gend = jnp.cumsum(counts) * row_len
    gstart = gend - counts * row_len
    row_readout = lax.dynamic_slice_in_dim(readout, mod_index * channels, channels, axis=0)
    projected_sorted = encode_rows(
        x, sorted_targets, gstart.astype(jnp.int32), gend.astype(jnp.int32),
        tin_all, tout_all, cin_all, cout_all, row_readout,
    )
    projected_part = jnp.take(projected_sorted, rank, axis=0)

    packed = jnp.concatenate(
        [
            projected_part.reshape(module_count, -1),
            veto_part.reshape(module_count, -1),
        ],
        axis=1,
    )
    width = packed.shape[1]
    lanes = 128
    padded = -(-width // (8 * lanes)) * 8 * lanes
    packed = jnp.pad(packed, ((0, 0), (0, padded - width)))
    totals = exchange_sum(packed.reshape(module_count, -1, lanes)).reshape(-1)
    split = projected_part.size // module_count
    projected = totals[:split].reshape(-1, channels)
    veto = totals[split:width]
    latent = rms_norm(projected) * latent_gain
    class_scores = jnp.dot(latent, class_weight, precision=lax.Precision.HIGHEST)
    return (veto[None], latent[None], class_scores[None])


def solution(mesh):
    in_specs = (
        P("stream", None, "mod", None),
        P(),
        P(),
        P("stream", None),
        P("stream", None, None),
        P("stream", None, None),
        P("stream", None, None),
        P("stream", None, None),
        P("stream", None, None),
        P(),
        P(),
        P(),
    )
    out_specs = (P("stream", "mod"), P("stream", "mod", None), P("stream", "mod", None))
    return jax.shard_map(local, mesh=mesh, in_specs=in_specs, out_specs=out_specs, check_vma=False)
```

```python
import functools

import jax
import jax.numpy as jnp
from jax import lax
from jax.experimental import pallas as pl
from jax.experimental.pallas import tpu as pltpu
from jax.sharding import PartitionSpec as P

PATCH = 16
BLOCK_HITS = 16


def rms_norm(values):
    return values * lax.rsqrt(jnp.mean(values * values, axis=-1, keepdims=True) + 1e-06)


def stem_layer(frame_pixels, stem_weight):
    count, height, width = frame_pixels.shape
    pixel_tiles = frame_pixels.reshape(count, height // PATCH, PATCH, width // PATCH, PATCH)
    kernel = stem_weight.reshape(PATCH, PATCH, -1)
    response = jnp.einsum(
        "fapbq,pqc->fabc", pixel_tiles, kernel, preferred_element_type=jnp.float32
    )
    return jax.nn.gelu(response).astype(jnp.bfloat16).reshape(count, -1, kernel.shape[-1])


def encoder_kernel(
    tgt_ref, gstart_ref, gend_ref,
    x_ref, tin_ref, tout_ref, cin_ref, cout_ref, ro_ref,
    o_ref, mix_scr, hid_scr, out_scr,
):
    f32, bf16 = jnp.float32, jnp.bfloat16
    block = pl.program_id(0)
    hits, row_len, channels = x_ref.shape
    groups = cin_ref.shape[0]
    base = block * hits
    for h in range(hits):
        t = tgt_ref[base + h]
        xh = x_ref[h].astype(f32)
        normed = rms_norm(xh).astype(bf16)
        pre = jnp.dot(tin_ref[t], normed, preferred_element_type=f32)
        mixed = jax.nn.gelu(pre).astype(bf16)
        mix = jnp.dot(tout_ref[t], mixed, preferred_element_type=f32)
        mix_scr[h * row_len:(h + 1) * row_len, :] = (xh + mix).astype(bf16).astype(f32)
    after_mix = mix_scr[...]
    normed_two = rms_norm(after_mix).astype(bf16)
    token = base * row_len + lax.broadcasted_iota(jnp.int32, (hits * row_len, 1), 0)
    first = tgt_ref[base]
    last = tgt_ref[base + hits - 1]
    for g in range(groups):
        @pl.when((g >= first) & (g <= last))
        def _():
            inside = (token >= gstart_ref[g]) & (token < gend_ref[g])
            part = jnp.dot(normed_two, cin_ref[g], preferred_element_type=f32)
            hid_scr[...] = jnp.where(inside, part, hid_scr[...])
    hidden = jax.nn.gelu(hid_scr[...]).astype(bf16)
    for g in range(groups):
        @pl.when((g >= first) & (g <= last))
        def _():
            inside = (token >= gstart_ref[g]) & (token < gend_ref[g])
            part = jnp.dot(hidden, cout_ref[g], preferred_element_type=f32)
            out_scr[...] = jnp.where(inside, part, out_scr[...])
    after_mlp = after_mix + out_scr[...]
    pooled = jnp.mean(after_mlp.reshape(hits, row_len, channels), axis=1).astype(bf16)
    o_ref[...] = jnp.dot(pooled, ro_ref[...], preferred_element_type=f32)


def encode_rows(x, sorted_targets, gstart, gend, tin_all, tout_all, cin_all, cout_all, row_readout):
    hit_count, row_len, channels = x.shape
    steps = hit_count // BLOCK_HITS
    full = lambda a: pl.BlockSpec(a.shape, lambda i, *_: (0,) * a.ndim)
    grid_spec = pltpu.PrefetchScalarGridSpec(
        num_scalar_prefetch=3,
        grid=(steps,),
        in_specs=[
            pl.BlockSpec((BLOCK_HITS, row_len, channels), lambda i, *_: (i, 0, 0)),
            full(tin_all),
            full(tout_all),
            full(cin_all),
            full(cout_all),
            full(row_readout),
        ],
        out_specs=pl.BlockSpec((BLOCK_HITS, channels), lambda i, *_: (i, 0)),
        scratch_shapes=[
            pltpu.VMEM((BLOCK_HITS * row_len, channels), jnp.float32),
            pltpu.VMEM((BLOCK_HITS * row_len, cin_all.shape[-1]), jnp.float32),
            pltpu.VMEM((BLOCK_HITS * row_len, channels), jnp.float32),
        ],
    )
    return pl.pallas_call(
        encoder_kernel,
        grid_spec=grid_spec,
        out_shape=jax.ShapeDtypeStruct((hit_count, channels), jnp.float32),
        compiler_params=pltpu.CompilerParams(dimension_semantics=("arbitrary",)),
    )(sorted_targets, gstart, gend, x, tin_all, tout_all, cin_all, cout_all, row_readout)


def exchange_kernel(n, x_ref, o_ref, recv, send_sems, recv_sems):
    me = lax.axis_index("mod")
    stream = lax.axis_index("stream")
    barrier = pltpu.get_barrier_semaphore()
    for d in range(1, n):
        pl.semaphore_signal(
            barrier, inc=1, device_id=(stream, lax.rem(me + d, n)),
            device_id_type=pl.DeviceIdType.MESH,
        )
    pl.semaphore_wait(barrier, n - 1)
    copies = []
    for d in range(1, n):
        target = lax.rem(me + d, n)
        copy = pltpu.make_async_remote_copy(
            src_ref=x_ref.at[target],
            dst_ref=recv.at[d - 1],
            send_sem=send_sems.at[d - 1],
            recv_sem=recv_sems.at[d - 1],
            device_id=(stream, target),
            device_id_type=pl.DeviceIdType.MESH,
        )
        copy.start()
        copies.append(copy)
    for copy in copies:
        copy.wait()
    total = x_ref[me]
    for d in range(n - 1):
        total = total + recv[d]
    o_ref[...] = total


def exchange_sum(x):
    n = x.shape[0]
    return pl.pallas_call(
        functools.partial(exchange_kernel, n),
        out_shape=jax.ShapeDtypeStruct(x.shape[1:], x.dtype),
        in_specs=[pl.BlockSpec(memory_space=pltpu.VMEM)],
        out_specs=pl.BlockSpec(memory_space=pltpu.VMEM),
        scratch_shapes=[
            pltpu.VMEM((n - 1,) + x.shape[1:], x.dtype),
            pltpu.SemaphoreType.DMA((n - 1,)),
            pltpu.SemaphoreType.DMA((n - 1,)),
        ],
        compiler_params=pltpu.CompilerParams(collective_id=0, has_side_effects=True),
    )(x)


def local(
    pixels,
    stem_weight,
    veto_weight,
    hit_frames,
    assign,
    token_in,
    token_out,
    chan_in,
    chan_out,
    readout,
    latent_gain,
    class_weight,
):
    f32 = jnp.float32
    stream_count = lax.axis_size("stream")
    module_count = lax.axis_size("mod")
    mod_index = lax.axis_index("mod")

    pieces = (token_in[0], token_out[0], chan_in[0], chan_out[0])
    lanes, align = 128, 16
    blocks, spans, start = [], [], 0
    for w in pieces:
        rows = -(-(-(-w.size // lanes)) // align) * align
        blocks.append(jnp.pad(w.reshape(-1), (0, rows * lanes - w.size)).reshape(rows, lanes))
        spans.append((start, rows))
        start += rows
    gathered = lax.all_gather(jnp.concatenate(blocks, axis=0), "stream")
    weights = []
    for w, (first_row, rows) in zip(pieces, spans):
        part = gathered[:, first_row:first_row + rows, :].reshape(stream_count, -1)
        weights.append(part[:, :w.size].reshape((stream_count,) + w.shape))
    tin_all, tout_all, cin_all, cout_all = weights

    features = stem_layer(pixels[0], stem_weight)
    channels = features.shape[-1]
    row_len = features.shape[1]

    means = jnp.mean(features.astype(f32), axis=1)
    row_weight = lax.dynamic_slice_in_dim(veto_weight, mod_index, 1, axis=0)
    veto_part = jnp.sum(means * row_weight, axis=1)

    hits = hit_frames[0]
    targets = assign[0, :, 0].astype(jnp.int32)
    position = jnp.arange(targets.shape[0], dtype=jnp.int32)
    before = (targets[None, :] < targets[:, None]) | (
        (targets[None, :] == targets[:, None]) & (position[None, :] < position[:, None])
    )
    rank = jnp.sum(before.astype(jnp.int32), axis=1)
    picks = rank[None, :] == position[:, None]
    sorted_targets = jnp.sum(jnp.where(picks, targets[None, :], 0), axis=1)
    sorted_frames = jnp.sum(jnp.where(picks, hits[None, :], 0), axis=1)
    x = jnp.take(features, sorted_frames, axis=0)
    counts = jnp.sum(
        (targets[None, :] == jnp.arange(stream_count, dtype=jnp.int32)[:, None]).astype(jnp.int32),
        axis=1,
    )
    gend = jnp.cumsum(counts) * row_len
    gstart = gend - counts * row_len
    row_readout = lax.dynamic_slice_in_dim(readout, mod_index * channels, channels, axis=0)
    projected_sorted = encode_rows(
        x, sorted_targets, gstart.astype(jnp.int32), gend.astype(jnp.int32),
        tin_all, tout_all, cin_all, cout_all, row_readout,
    )
    projected_part = jnp.take(projected_sorted, rank, axis=0)

    packed = jnp.concatenate(
        [
            projected_part.reshape(module_count, -1),
            veto_part.reshape(module_count, -1),
        ],
        axis=1,
    )
    width = packed.shape[1]
    lanes = 128
    padded = -(-width // (8 * lanes)) * 8 * lanes
    packed = jnp.pad(packed, ((0, 0), (0, padded - width)))
    totals = exchange_sum(packed.reshape(module_count, -1, lanes)).reshape(-1)
    split = projected_part.size // module_count
    projected = totals[:split].reshape(-1, channels)
    veto = totals[split:width]
    latent = rms_norm(projected) * latent_gain
    class_scores = jnp.dot(latent, class_weight, precision=lax.Precision.HIGHEST)
    return (veto[None], latent[None], class_scores[None])


def solution(mesh):
    in_specs = (
        P("stream", None, "mod", None),
        P(),
        P(),
        P("stream", None),
        P("stream", None, None),
        P("stream", None, None),
        P("stream", None, None),
        P("stream", None, None),
        P("stream", None, None),
        P(),
        P(),
        P(),
    )
    out_specs = (P("stream", "mod"), P("stream", "mod", None), P("stream", "mod", None))
    return jax.shard_map(local, mesh=mesh, in_specs=in_specs, out_specs=out_specs, check_vma=False)
```

```python
import functools

import jax
import jax.numpy as jnp
from jax import lax
from jax.experimental import pallas as pl
from jax.experimental.pallas import tpu as pltpu
from jax.sharding import PartitionSpec as P

PATCH = 16
BLOCK_HITS = 16


def rms_norm(values):
    return values * lax.rsqrt(jnp.mean(values * values, axis=-1, keepdims=True) + 1e-06)


def stem_layer(frame_pixels, stem_weight):
    count, height, width = frame_pixels.shape
    pixel_tiles = frame_pixels.reshape(count, height // PATCH, PATCH, width // PATCH, PATCH)
    kernel = stem_weight.reshape(PATCH, PATCH, -1)
    response = jnp.einsum(
        "fapbq,pqc->fabc", pixel_tiles, kernel, preferred_element_type=jnp.float32
    )
    return jax.nn.gelu(response).astype(jnp.bfloat16).reshape(count, -1, kernel.shape[-1])


def encoder_kernel(
    tgt_ref, gstart_ref, gend_ref,
    x_ref, tin_ref, tout_ref, cin_ref, cout_ref, ro_ref,
    o_ref, mix_scr, hid_scr, out_scr,
):
    f32, bf16 = jnp.float32, jnp.bfloat16
    block = pl.program_id(0)
    hits, row_len, channels = x_ref.shape
    groups = cin_ref.shape[0]
    base = block * hits
    for h in range(hits):
        t = tgt_ref[base + h]
        xh = x_ref[h].astype(f32)
        normed = rms_norm(xh).astype(bf16)
        pre = jnp.dot(tin_ref[t], normed, preferred_element_type=f32)
        mixed = jax.nn.gelu(pre).astype(bf16)
        mix = jnp.dot(tout_ref[t], mixed, preferred_element_type=f32)
        mix_scr[h * row_len:(h + 1) * row_len, :] = (xh + mix).astype(bf16).astype(f32)
    after_mix = mix_scr[...]
    normed_two = rms_norm(after_mix).astype(bf16)
    token = base * row_len + lax.broadcasted_iota(jnp.int32, (hits * row_len, 1), 0)
    first = tgt_ref[base]
    last = tgt_ref[base + hits - 1]
    head = token < gend_ref[first]
    hid_scr[...] = jnp.where(
        head,
        jnp.dot(normed_two, cin_ref[first], preferred_element_type=f32),
        jnp.dot(normed_two, cin_ref[last], preferred_element_type=f32),
    )
    for g in range(groups):
        @pl.when((g > first) & (g < last))
        def _():
            inside = (token >= gstart_ref[g]) & (token < gend_ref[g])
            part = jnp.dot(normed_two, cin_ref[g], preferred_element_type=f32)
            hid_scr[...] = jnp.where(inside, part, hid_scr[...])
    hidden = jax.nn.gelu(hid_scr[...]).astype(bf16)
    out_scr[...] = jnp.where(
        head,
        jnp.dot(hidden, cout_ref[first], preferred_element_type=f32),
        jnp.dot(hidden, cout_ref[last], preferred_element_type=f32),
    )
    for g in range(groups):
        @pl.when((g > first) & (g < last))
        def _():
            inside = (token >= gstart_ref[g]) & (token < gend_ref[g])
            part = jnp.dot(hidden, cout_ref[g], preferred_element_type=f32)
            out_scr[...] = jnp.where(inside, part, out_scr[...])
    after_mlp = after_mix + out_scr[...]
    pooled = jnp.mean(after_mlp.reshape(hits, row_len, channels), axis=1).astype(bf16)
    o_ref[...] = jnp.dot(pooled, ro_ref[...], preferred_element_type=f32)


def encode_rows(x, sorted_targets, gstart, gend, tin_all, tout_all, cin_all, cout_all, row_readout):
    hit_count, row_len, channels = x.shape
    steps = hit_count // BLOCK_HITS
    full = lambda a: pl.BlockSpec(a.shape, lambda i, *_: (0,) * a.ndim)
    grid_spec = pltpu.PrefetchScalarGridSpec(
        num_scalar_prefetch=3,
        grid=(steps,),
        in_specs=[
            pl.BlockSpec((BLOCK_HITS, row_len, channels), lambda i, *_: (i, 0, 0)),
            full(tin_all),
            full(tout_all),
            full(cin_all),
            full(cout_all),
            full(row_readout),
        ],
        out_specs=pl.BlockSpec((BLOCK_HITS, channels), lambda i, *_: (i, 0)),
        scratch_shapes=[
            pltpu.VMEM((BLOCK_HITS * row_len, channels), jnp.float32),
            pltpu.VMEM((BLOCK_HITS * row_len, cin_all.shape[-1]), jnp.float32),
            pltpu.VMEM((BLOCK_HITS * row_len, channels), jnp.float32),
        ],
    )
    return pl.pallas_call(
        encoder_kernel,
        grid_spec=grid_spec,
        out_shape=jax.ShapeDtypeStruct((hit_count, channels), jnp.float32),
        compiler_params=pltpu.CompilerParams(dimension_semantics=("arbitrary",)),
    )(sorted_targets, gstart, gend, x, tin_all, tout_all, cin_all, cout_all, row_readout)


def exchange_kernel(n, x_ref, o_ref, recv, send_sems, recv_sems):
    me = lax.axis_index("mod")
    stream = lax.axis_index("stream")
    barrier = pltpu.get_barrier_semaphore()
    for d in range(1, n):
        pl.semaphore_signal(
            barrier, inc=1, device_id=(stream, lax.rem(me + d, n)),
            device_id_type=pl.DeviceIdType.MESH,
        )
    pl.semaphore_wait(barrier, n - 1)
    copies = []
    for d in range(1, n):
        target = lax.rem(me + d, n)
        copy = pltpu.make_async_remote_copy(
            src_ref=x_ref.at[target],
            dst_ref=recv.at[d - 1],
            send_sem=send_sems.at[d - 1],
            recv_sem=recv_sems.at[d - 1],
            device_id=(stream, target),
            device_id_type=pl.DeviceIdType.MESH,
        )
        copy.start()
        copies.append(copy)
    for copy in copies:
        copy.wait()
    total = x_ref[me]
    for d in range(n - 1):
        total = total + recv[d]
    o_ref[...] = total


def exchange_sum(x):
    n = x.shape[0]
    return pl.pallas_call(
        functools.partial(exchange_kernel, n),
        out_shape=jax.ShapeDtypeStruct(x.shape[1:], x.dtype),
        in_specs=[pl.BlockSpec(memory_space=pltpu.VMEM)],
        out_specs=pl.BlockSpec(memory_space=pltpu.VMEM),
        scratch_shapes=[
            pltpu.VMEM((n - 1,) + x.shape[1:], x.dtype),
            pltpu.SemaphoreType.DMA((n - 1,)),
            pltpu.SemaphoreType.DMA((n - 1,)),
        ],
        compiler_params=pltpu.CompilerParams(collective_id=0, has_side_effects=True),
    )(x)


def local(
    pixels,
    stem_weight,
    veto_weight,
    hit_frames,
    assign,
    token_in,
    token_out,
    chan_in,
    chan_out,
    readout,
    latent_gain,
    class_weight,
):
    f32 = jnp.float32
    stream_count = lax.axis_size("stream")
    module_count = lax.axis_size("mod")
    mod_index = lax.axis_index("mod")

    pieces = (token_in[0], token_out[0], chan_in[0], chan_out[0])
    lanes, align = 128, 16
    blocks, spans, start = [], [], 0
    for w in pieces:
        rows = -(-(-(-w.size // lanes)) // align) * align
        blocks.append(jnp.pad(w.reshape(-1), (0, rows * lanes - w.size)).reshape(rows, lanes))
        spans.append((start, rows))
        start += rows
    gathered = lax.all_gather(jnp.concatenate(blocks, axis=0), "stream")
    weights = []
    for w, (first_row, rows) in zip(pieces, spans):
        part = gathered[:, first_row:first_row + rows, :].reshape(stream_count, -1)
        weights.append(part[:, :w.size].reshape((stream_count,) + w.shape))
    tin_all, tout_all, cin_all, cout_all = weights

    features = stem_layer(pixels[0], stem_weight)
    channels = features.shape[-1]
    row_len = features.shape[1]

    means = jnp.mean(features.astype(f32), axis=1)
    row_weight = lax.dynamic_slice_in_dim(veto_weight, mod_index, 1, axis=0)
    veto_part = jnp.sum(means * row_weight, axis=1)

    hits = hit_frames[0]
    targets = assign[0, :, 0].astype(jnp.int32)
    position = jnp.arange(targets.shape[0], dtype=jnp.int32)
    before = (targets[None, :] < targets[:, None]) | (
        (targets[None, :] == targets[:, None]) & (position[None, :] < position[:, None])
    )
    rank = jnp.sum(before.astype(jnp.int32), axis=1)
    picks = rank[None, :] == position[:, None]
    sorted_targets = jnp.sum(jnp.where(picks, targets[None, :], 0), axis=1)
    sorted_frames = jnp.sum(jnp.where(picks, hits[None, :], 0), axis=1)
    x = jnp.take(features, sorted_frames, axis=0)
    counts = jnp.sum(
        (targets[None, :] == jnp.arange(stream_count, dtype=jnp.int32)[:, None]).astype(jnp.int32),
        axis=1,
    )
    gend = jnp.cumsum(counts) * row_len
    gstart = gend - counts * row_len
    row_readout = lax.dynamic_slice_in_dim(readout, mod_index * channels, channels, axis=0)
    projected_sorted = encode_rows(
        x, sorted_targets, gstart.astype(jnp.int32), gend.astype(jnp.int32),
        tin_all, tout_all, cin_all, cout_all, row_readout,
    )
    projected_part = jnp.take(projected_sorted, rank, axis=0)

    packed = jnp.concatenate(
        [
            projected_part.reshape(module_count, -1),
            veto_part.reshape(module_count, -1),
        ],
        axis=1,
    )
    width = packed.shape[1]
    lanes = 128
    padded = -(-width // (8 * lanes)) * 8 * lanes
    packed = jnp.pad(packed, ((0, 0), (0, padded - width)))
    totals = exchange_sum(packed.reshape(module_count, -1, lanes)).reshape(-1)
    split = projected_part.size // module_count
    projected = totals[:split].reshape(-1, channels)
    veto = totals[split:width]
    latent = rms_norm(projected) * latent_gain
    class_scores = jnp.dot(latent, class_weight, precision=lax.Precision.HIGHEST)
    return (veto[None], latent[None], class_scores[None])


def solution(mesh):
    in_specs = (
        P("stream", None, "mod", None),
        P(),
        P(),
        P("stream", None),
        P("stream", None, None),
        P("stream", None, None),
        P("stream", None, None),
        P("stream", None, None),
        P("stream", None, None),
        P(),
        P(),
        P(),
    )
    out_specs = (P("stream", "mod"), P("stream", "mod", None), P("stream", "mod", None))
    return jax.shard_map(local, mesh=mesh, in_specs=in_specs, out_specs=out_specs, check_vma=False)
```

```python
import functools

import jax
import jax.numpy as jnp
from jax import lax
from jax.experimental import pallas as pl
from jax.experimental.pallas import tpu as pltpu
from jax.sharding import PartitionSpec as P

PATCH = 16
BLOCK_HITS = 16


def rms_norm(values):
    return values * lax.rsqrt(jnp.mean(values * values, axis=-1, keepdims=True) + 1e-06)


def stem_layer(frame_pixels, stem_weight):
    count, height, width = frame_pixels.shape
    pixel_tiles = frame_pixels.reshape(count, height // PATCH, PATCH, width // PATCH, PATCH)
    kernel = stem_weight.reshape(PATCH, PATCH, -1)
    response = jnp.einsum(
        "fapbq,pqc->fabc", pixel_tiles, kernel, preferred_element_type=jnp.float32
    )
    return jax.nn.gelu(response).astype(jnp.bfloat16).reshape(count, -1, kernel.shape[-1])


def gelu_tanh(x):
    k = 0.7978845608028654
    inner = x * (k + (k * 0.044715) * (x * x))
    half = 0.5 * x
    return half + half * jnp.tanh(inner)


def encoder_kernel(
    tgt_ref, gstart_ref, gend_ref,
    x_ref, tin_ref, tout_ref, cin_ref, cout_ref, ro_ref,
    o_ref, mix_scr, hid_scr, out_scr,
):
    f32, bf16 = jnp.float32, jnp.bfloat16
    block = pl.program_id(0)
    hits, row_len, channels = x_ref.shape
    groups = cin_ref.shape[0]
    base = block * hits
    for h in range(hits):
        t = tgt_ref[base + h]
        xh = x_ref[h].astype(f32)
        normed = rms_norm(xh).astype(bf16)
        pre = jnp.dot(tin_ref[t], normed, preferred_element_type=f32)
        mixed = gelu_tanh(pre.astype(bf16)).astype(bf16)
        mix = jnp.dot(tout_ref[t], mixed, preferred_element_type=f32)
        mix_scr[h * row_len:(h + 1) * row_len, :] = (xh + mix).astype(bf16).astype(f32)
    after_mix = mix_scr[...]
    normed_two = rms_norm(after_mix).astype(bf16)
    token = base * row_len + lax.broadcasted_iota(jnp.int32, (hits * row_len, 1), 0)
    first = tgt_ref[base]
    last = tgt_ref[base + hits - 1]
    head = token < gend_ref[first]
    hid_scr[...] = jnp.where(
        head,
        jnp.dot(normed_two, cin_ref[first], preferred_element_type=f32),
        jnp.dot(normed_two, cin_ref[last], preferred_element_type=f32),
    )
    for g in range(groups):
        @pl.when((g > first) & (g < last))
        def _():
            inside = (token >= gstart_ref[g]) & (token < gend_ref[g])
            part = jnp.dot(normed_two, cin_ref[g], preferred_element_type=f32)
            hid_scr[...] = jnp.where(inside, part, hid_scr[...])
    hidden = jax.nn.gelu(hid_scr[...]).astype(bf16)
    out_scr[...] = jnp.where(
        head,
        jnp.dot(hidden, cout_ref[first], preferred_element_type=f32),
        jnp.dot(hidden, cout_ref[last], preferred_element_type=f32),
    )
    for g in range(groups):
        @pl.when((g > first) & (g < last))
        def _():
            inside = (token >= gstart_ref[g]) & (token < gend_ref[g])
            part = jnp.dot(hidden, cout_ref[g], preferred_element_type=f32)
            out_scr[...] = jnp.where(inside, part, out_scr[...])
    after_mlp = after_mix + out_scr[...]
    pooled = jnp.mean(after_mlp.reshape(hits, row_len, channels), axis=1).astype(bf16)
    o_ref[...] = jnp.dot(pooled, ro_ref[...], preferred_element_type=f32)


def encode_rows(x, sorted_targets, gstart, gend, tin_all, tout_all, cin_all, cout_all, row_readout):
    hit_count, row_len, channels = x.shape
    steps = hit_count // BLOCK_HITS
    full = lambda a: pl.BlockSpec(a.shape, lambda i, *_: (0,) * a.ndim)
    grid_spec = pltpu.PrefetchScalarGridSpec(
        num_scalar_prefetch=3,
        grid=(steps,),
        in_specs=[
            pl.BlockSpec((BLOCK_HITS, row_len, channels), lambda i, *_: (i, 0, 0)),
            full(tin_all),
            full(tout_all),
            full(cin_all),
            full(cout_all),
            full(row_readout),
        ],
        out_specs=pl.BlockSpec((BLOCK_HITS, channels), lambda i, *_: (i, 0)),
        scratch_shapes=[
            pltpu.VMEM((BLOCK_HITS * row_len, channels), jnp.float32),
            pltpu.VMEM((BLOCK_HITS * row_len, cin_all.shape[-1]), jnp.float32),
            pltpu.VMEM((BLOCK_HITS * row_len, channels), jnp.float32),
        ],
    )
    return pl.pallas_call(
        encoder_kernel,
        grid_spec=grid_spec,
        out_shape=jax.ShapeDtypeStruct((hit_count, channels), jnp.float32),
        compiler_params=pltpu.CompilerParams(dimension_semantics=("arbitrary",)),
    )(sorted_targets, gstart, gend, x, tin_all, tout_all, cin_all, cout_all, row_readout)


def exchange_kernel(n, x_ref, o_ref, recv, send_sems, recv_sems):
    me = lax.axis_index("mod")
    stream = lax.axis_index("stream")
    barrier = pltpu.get_barrier_semaphore()
    for d in range(1, n):
        pl.semaphore_signal(
            barrier, inc=1, device_id=(stream, lax.rem(me + d, n)),
            device_id_type=pl.DeviceIdType.MESH,
        )
    pl.semaphore_wait(barrier, n - 1)
    copies = []
    for d in range(1, n):
        target = lax.rem(me + d, n)
        copy = pltpu.make_async_remote_copy(
            src_ref=x_ref.at[target],
            dst_ref=recv.at[d - 1],
            send_sem=send_sems.at[d - 1],
            recv_sem=recv_sems.at[d - 1],
            device_id=(stream, target),
            device_id_type=pl.DeviceIdType.MESH,
        )
        copy.start()
        copies.append(copy)
    for copy in copies:
        copy.wait()
    total = x_ref[me]
    for d in range(n - 1):
        total = total + recv[d]
    o_ref[...] = total


def exchange_sum(x):
    n = x.shape[0]
    return pl.pallas_call(
        functools.partial(exchange_kernel, n),
        out_shape=jax.ShapeDtypeStruct(x.shape[1:], x.dtype),
        in_specs=[pl.BlockSpec(memory_space=pltpu.VMEM)],
        out_specs=pl.BlockSpec(memory_space=pltpu.VMEM),
        scratch_shapes=[
            pltpu.VMEM((n - 1,) + x.shape[1:], x.dtype),
            pltpu.SemaphoreType.DMA((n - 1,)),
            pltpu.SemaphoreType.DMA((n - 1,)),
        ],
        compiler_params=pltpu.CompilerParams(collective_id=0, has_side_effects=True),
    )(x)


def local(
    pixels,
    stem_weight,
    veto_weight,
    hit_frames,
    assign,
    token_in,
    token_out,
    chan_in,
    chan_out,
    readout,
    latent_gain,
    class_weight,
):
    f32 = jnp.float32
    stream_count = lax.axis_size("stream")
    module_count = lax.axis_size("mod")
    mod_index = lax.axis_index("mod")

    pieces = (token_in[0], token_out[0], chan_in[0], chan_out[0])
    lanes, align = 128, 16
    blocks, spans, start = [], [], 0
    for w in pieces:
        rows = -(-(-(-w.size // lanes)) // align) * align
        blocks.append(jnp.pad(w.reshape(-1), (0, rows * lanes - w.size)).reshape(rows, lanes))
        spans.append((start, rows))
        start += rows
    gathered = lax.all_gather(jnp.concatenate(blocks, axis=0), "stream")
    weights = []
    for w, (first_row, rows) in zip(pieces, spans):
        part = gathered[:, first_row:first_row + rows, :].reshape(stream_count, -1)
        weights.append(part[:, :w.size].reshape((stream_count,) + w.shape))
    tin_all, tout_all, cin_all, cout_all = weights

    features = stem_layer(pixels[0], stem_weight)
    channels = features.shape[-1]
    row_len = features.shape[1]

    means = jnp.mean(features.astype(f32), axis=1)
    row_weight = lax.dynamic_slice_in_dim(veto_weight, mod_index, 1, axis=0)
    veto_part = jnp.sum(means * row_weight, axis=1)

    hits = hit_frames[0]
    targets = assign[0, :, 0].astype(jnp.int32)
    position = jnp.arange(targets.shape[0], dtype=jnp.int32)
    before = (targets[None, :] < targets[:, None]) | (
        (targets[None, :] == targets[:, None]) & (position[None, :] < position[:, None])
    )
    rank = jnp.sum(before.astype(jnp.int32), axis=1)
    picks = rank[None, :] == position[:, None]
    sorted_targets = jnp.sum(jnp.where(picks, targets[None, :], 0), axis=1)
    sorted_frames = jnp.sum(jnp.where(picks, hits[None, :], 0), axis=1)
    x = jnp.take(features, sorted_frames, axis=0)
    counts = jnp.sum(
        (targets[None, :] == jnp.arange(stream_count, dtype=jnp.int32)[:, None]).astype(jnp.int32),
        axis=1,
    )
    gend = jnp.cumsum(counts) * row_len
    gstart = gend - counts * row_len
    row_readout = lax.dynamic_slice_in_dim(readout, mod_index * channels, channels, axis=0)
    projected_sorted = encode_rows(
        x, sorted_targets, gstart.astype(jnp.int32), gend.astype(jnp.int32),
        tin_all, tout_all, cin_all, cout_all, row_readout,
    )
    projected_part = jnp.take(projected_sorted, rank, axis=0)

    packed = jnp.concatenate(
        [
            projected_part.reshape(module_count, -1),
            veto_part.reshape(module_count, -1),
        ],
        axis=1,
    )
    width = packed.shape[1]
    lanes = 128
    padded = -(-width // (8 * lanes)) * 8 * lanes
    packed = jnp.pad(packed, ((0, 0), (0, padded - width)))
    totals = exchange_sum(packed.reshape(module_count, -1, lanes)).reshape(-1)
    split = projected_part.size // module_count
    projected = totals[:split].reshape(-1, channels)
    veto = totals[split:width]
    latent = rms_norm(projected) * latent_gain
    class_scores = jnp.dot(latent, class_weight, precision=lax.Precision.HIGHEST)
    return (veto[None], latent[None], class_scores[None])


def solution(mesh):
    in_specs = (
        P("stream", None, "mod", None),
        P(),
        P(),
        P("stream", None),
        P("stream", None, None),
        P("stream", None, None),
        P("stream", None, None),
        P("stream", None, None),
        P("stream", None, None),
        P(),
        P(),
        P(),
    )
    out_specs = (P("stream", "mod"), P("stream", "mod", None), P("stream", "mod", None))
    return jax.shard_map(local, mesh=mesh, in_specs=in_specs, out_specs=out_specs, check_vma=False)
```

```python
import functools

import jax
import jax.numpy as jnp
from jax import lax
from jax.experimental import pallas as pl
from jax.experimental.pallas import tpu as pltpu
from jax.sharding import PartitionSpec as P

PATCH = 16
BLOCK_HITS = 16


def rms_norm(values):
    return values * lax.rsqrt(jnp.mean(values * values, axis=-1, keepdims=True) + 1e-06)


def stem_layer(frame_pixels, stem_weight):
    count, height, width = frame_pixels.shape
    pixel_tiles = frame_pixels.reshape(count, height // PATCH, PATCH, width // PATCH, PATCH)
    kernel = stem_weight.reshape(PATCH, PATCH, -1)
    response = jnp.einsum(
        "fapbq,pqc->fabc", pixel_tiles, kernel, preferred_element_type=jnp.float32
    )
    return jax.nn.gelu(response).astype(jnp.bfloat16).reshape(count, -1, kernel.shape[-1])


def gelu_tanh(x):
    k = 0.7978845608028654
    inner = x * (k + (k * 0.044715) * (x * x))
    half = 0.5 * x
    return half + half * jnp.tanh(inner)


def encoder_kernel(
    tgt_ref, gstart_ref, gend_ref,
    x_ref, tin_ref, tout_ref, cin_ref, cout_ref, ro_ref,
    o_ref, mix_scr, hid_scr, out_scr,
):
    f32, bf16 = jnp.float32, jnp.bfloat16
    block = pl.program_id(0)
    hits, row_len, channels = x_ref.shape
    groups = cin_ref.shape[0]
    base = block * hits
    for h in range(hits):
        t = tgt_ref[base + h]
        xh = x_ref[h].astype(f32)
        normed = rms_norm(xh).astype(bf16)
        pre = jnp.dot(tin_ref[t], normed, preferred_element_type=f32)
        mixed = gelu_tanh(pre.astype(bf16)).astype(bf16)
        mix = jnp.dot(tout_ref[t], mixed, preferred_element_type=f32)
        mix_scr[h * row_len:(h + 1) * row_len, :] = (xh + mix).astype(bf16).astype(f32)
    after_mix = mix_scr[...]
    normed_two = rms_norm(after_mix).astype(bf16)
    token = base * row_len + lax.broadcasted_iota(jnp.int32, (hits * row_len, 1), 0)
    first = tgt_ref[base]
    last = tgt_ref[base + hits - 1]
    head = token < gend_ref[first]
    hid_scr[...] = jnp.where(
        head,
        jnp.dot(normed_two, cin_ref[first], preferred_element_type=f32),
        jnp.dot(normed_two, cin_ref[last], preferred_element_type=f32),
    )
    for g in range(groups):
        @pl.when((g > first) & (g < last))
        def _():
            inside = (token >= gstart_ref[g]) & (token < gend_ref[g])
            part = jnp.dot(normed_two, cin_ref[g], preferred_element_type=f32)
            hid_scr[...] = jnp.where(inside, part, hid_scr[...])
    hidden = jax.nn.gelu(hid_scr[...]).astype(bf16)
    out_scr[...] = jnp.where(
        head,
        jnp.dot(hidden, cout_ref[first], preferred_element_type=f32),
        jnp.dot(hidden, cout_ref[last], preferred_element_type=f32),
    )
    for g in range(groups):
        @pl.when((g > first) & (g < last))
        def _():
            inside = (token >= gstart_ref[g]) & (token < gend_ref[g])
            part = jnp.dot(hidden, cout_ref[g], preferred_element_type=f32)
            out_scr[...] = jnp.where(inside, part, out_scr[...])
    after_mlp = after_mix + out_scr[...]
    pooled = jnp.mean(after_mlp.reshape(hits, row_len, channels), axis=1).astype(bf16)
    o_ref[...] = jnp.dot(pooled, ro_ref[...], preferred_element_type=f32)


def encode_rows(x, sorted_targets, gstart, gend, tin_all, tout_all, cin_all, cout_all, row_readout):
    hit_count, row_len, channels = x.shape
    steps = hit_count // BLOCK_HITS
    full = lambda a: pl.BlockSpec(a.shape, lambda i, *_: (0,) * a.ndim)
    grid_spec = pltpu.PrefetchScalarGridSpec(
        num_scalar_prefetch=3,
        grid=(steps,),
        in_specs=[
            pl.BlockSpec((BLOCK_HITS, row_len, channels), lambda i, *_: (i, 0, 0)),
            full(tin_all),
            full(tout_all),
            full(cin_all),
            full(cout_all),
            full(row_readout),
        ],
        out_specs=pl.BlockSpec((BLOCK_HITS, channels), lambda i, *_: (i, 0)),
        scratch_shapes=[
            pltpu.VMEM((BLOCK_HITS * row_len, channels), jnp.float32),
            pltpu.VMEM((BLOCK_HITS * row_len, cin_all.shape[-1]), jnp.float32),
            pltpu.VMEM((BLOCK_HITS * row_len, channels), jnp.float32),
        ],
    )
    return pl.pallas_call(
        encoder_kernel,
        grid_spec=grid_spec,
        out_shape=jax.ShapeDtypeStruct((hit_count, channels), jnp.float32),
        compiler_params=pltpu.CompilerParams(dimension_semantics=("arbitrary",)),
    )(sorted_targets, gstart, gend, x, tin_all, tout_all, cin_all, cout_all, row_readout)


def exchange_kernel(n, x_ref, o_ref, recv, send_sems, recv_sems):
    me = lax.axis_index("mod")
    stream = lax.axis_index("stream")
    barrier = pltpu.get_barrier_semaphore()
    for d in range(1, n):
        pl.semaphore_signal(
            barrier, inc=1, device_id=(stream, lax.rem(me + d, n)),
            device_id_type=pl.DeviceIdType.MESH,
        )
    pl.semaphore_wait(barrier, n - 1)
    copies = []
    for d in range(1, n):
        target = lax.rem(me + d, n)
        copy = pltpu.make_async_remote_copy(
            src_ref=x_ref.at[target],
            dst_ref=recv.at[d - 1],
            send_sem=send_sems.at[d - 1],
            recv_sem=recv_sems.at[d - 1],
            device_id=(stream, target),
            device_id_type=pl.DeviceIdType.MESH,
        )
        copy.start()
        copies.append(copy)
    for copy in copies:
        copy.wait()
    total = x_ref[me]
    for d in range(n - 1):
        total = total + recv[d]
    o_ref[...] = total


def exchange_sum(x):
    n = x.shape[0]
    return pl.pallas_call(
        functools.partial(exchange_kernel, n),
        out_shape=jax.ShapeDtypeStruct(x.shape[1:], x.dtype),
        in_specs=[pl.BlockSpec(memory_space=pltpu.VMEM)],
        out_specs=pl.BlockSpec(memory_space=pltpu.VMEM),
        scratch_shapes=[
            pltpu.VMEM((n - 1,) + x.shape[1:], x.dtype),
            pltpu.SemaphoreType.DMA((n - 1,)),
            pltpu.SemaphoreType.DMA((n - 1,)),
        ],
        compiler_params=pltpu.CompilerParams(collective_id=0, has_side_effects=True),
    )(x)


def local(
    pixels,
    stem_weight,
    veto_weight,
    hit_frames,
    assign,
    token_in,
    token_out,
    chan_in,
    chan_out,
    readout,
    latent_gain,
    class_weight,
):
    f32 = jnp.float32
    stream_count = lax.axis_size("stream")
    module_count = lax.axis_size("mod")
    mod_index = lax.axis_index("mod")

    pieces = (token_in[0], token_out[0], chan_in[0], chan_out[0])
    lanes, align = 128, 16
    blocks, spans, start = [], [], 0
    for w in pieces:
        rows = -(-(-(-w.size // lanes)) // align) * align
        blocks.append(jnp.pad(w.reshape(-1), (0, rows * lanes - w.size)).reshape(rows, lanes))
        spans.append((start, rows))
        start += rows
    gathered = lax.all_gather(jnp.concatenate(blocks, axis=0), "stream")
    weights = []
    for w, (first_row, rows) in zip(pieces, spans):
        part = gathered[:, first_row:first_row + rows, :].reshape(stream_count, -1)
        weights.append(part[:, :w.size].reshape((stream_count,) + w.shape))
    tin_all, tout_all, cin_all, cout_all = weights

    features = stem_layer(pixels[0], stem_weight)
    channels = features.shape[-1]
    row_len = features.shape[1]

    means = jnp.mean(features.astype(f32), axis=1)
    row_weight = lax.dynamic_slice_in_dim(veto_weight, mod_index, 1, axis=0)
    veto_part = jnp.sum(means * row_weight, axis=1)

    hits = hit_frames[0]
    targets = assign[0, :, 0].astype(jnp.int32)
    position = jnp.arange(targets.shape[0], dtype=jnp.int32)
    before = (targets[None, :] < targets[:, None]) | (
        (targets[None, :] == targets[:, None]) & (position[None, :] < position[:, None])
    )
    rank = jnp.sum(before.astype(jnp.int32), axis=1)
    picks = rank[None, :] == position[:, None]
    sorted_targets = jnp.sum(jnp.where(picks, targets[None, :], 0), axis=1)
    sorted_frames = jnp.sum(jnp.where(picks, hits[None, :], 0), axis=1)
    x = stem_layer(jnp.take(pixels[0], sorted_frames, axis=0), stem_weight)
    counts = jnp.sum(
        (targets[None, :] == jnp.arange(stream_count, dtype=jnp.int32)[:, None]).astype(jnp.int32),
        axis=1,
    )
    gend = jnp.cumsum(counts) * row_len
    gstart = gend - counts * row_len
    row_readout = lax.dynamic_slice_in_dim(readout, mod_index * channels, channels, axis=0)
    projected_sorted = encode_rows(
        x, sorted_targets, gstart.astype(jnp.int32), gend.astype(jnp.int32),
        tin_all, tout_all, cin_all, cout_all, row_readout,
    )
    projected_part = jnp.take(projected_sorted, rank, axis=0)

    packed = jnp.concatenate(
        [
            projected_part.reshape(module_count, -1),
            veto_part.reshape(module_count, -1),
        ],
        axis=1,
    )
    width = packed.shape[1]
    lanes = 128
    padded = -(-width // (8 * lanes)) * 8 * lanes
    packed = jnp.pad(packed, ((0, 0), (0, padded - width)))
    totals = exchange_sum(packed.reshape(module_count, -1, lanes)).reshape(-1)
    split = projected_part.size // module_count
    projected = totals[:split].reshape(-1, channels)
    veto = totals[split:width]
    latent = rms_norm(projected) * latent_gain
    class_scores = jnp.dot(latent, class_weight, precision=lax.Precision.HIGHEST)
    return (veto[None], latent[None], class_scores[None])


def solution(mesh):
    in_specs = (
        P("stream", None, "mod", None),
        P(),
        P(),
        P("stream", None),
        P("stream", None, None),
        P("stream", None, None),
        P("stream", None, None),
        P("stream", None, None),
        P("stream", None, None),
        P(),
        P(),
        P(),
    )
    out_specs = (P("stream", "mod"), P("stream", "mod", None), P("stream", "mod", None))
    return jax.shard_map(local, mesh=mesh, in_specs=in_specs, out_specs=out_specs, check_vma=False)
```

```python
import functools

import jax
import jax.numpy as jnp
from jax import lax
from jax.experimental import pallas as pl
from jax.experimental.pallas import tpu as pltpu
from jax.sharding import PartitionSpec as P

PATCH = 16
BLOCK_HITS = 32


def rms_norm(values):
    return values * lax.rsqrt(jnp.mean(values * values, axis=-1, keepdims=True) + 1e-06)


def stem_layer(frame_pixels, stem_weight):
    count, height, width = frame_pixels.shape
    pixel_tiles = frame_pixels.reshape(count, height // PATCH, PATCH, width // PATCH, PATCH)
    kernel = stem_weight.reshape(PATCH, PATCH, -1)
    response = jnp.einsum(
        "fapbq,pqc->fabc", pixel_tiles, kernel, preferred_element_type=jnp.float32
    )
    return jax.nn.gelu(response).astype(jnp.bfloat16).reshape(count, -1, kernel.shape[-1])


def gelu_tanh(x):
    k = 0.7978845608028654
    inner = x * (k + (k * 0.044715) * (x * x))
    half = 0.5 * x
    return half + half * jnp.tanh(inner)


def encoder_kernel(
    tgt_ref, gstart_ref, gend_ref,
    x_ref, tin_ref, tout_ref, cin_ref, cout_ref, ro_ref,
    o_ref, mix_scr, hid_scr, out_scr,
):
    f32, bf16 = jnp.float32, jnp.bfloat16
    block = pl.program_id(0)
    hits, row_len, channels = x_ref.shape
    groups = cin_ref.shape[0]
    base = block * hits
    for h in range(hits):
        t = tgt_ref[base + h]
        xh = x_ref[h].astype(f32)
        normed = rms_norm(xh).astype(bf16)
        pre = jnp.dot(tin_ref[t], normed, preferred_element_type=f32)
        mixed = gelu_tanh(pre.astype(bf16)).astype(bf16)
        mix = jnp.dot(tout_ref[t], mixed, preferred_element_type=f32)
        mix_scr[h * row_len:(h + 1) * row_len, :] = (xh + mix).astype(bf16).astype(f32)
    after_mix = mix_scr[...]
    normed_two = rms_norm(after_mix).astype(bf16)
    token = base * row_len + lax.broadcasted_iota(jnp.int32, (hits * row_len, 1), 0)
    first = tgt_ref[base]
    last = tgt_ref[base + hits - 1]
    head = token < gend_ref[first]
    hid_scr[...] = jnp.where(
        head,
        jnp.dot(normed_two, cin_ref[first], preferred_element_type=f32),
        jnp.dot(normed_two, cin_ref[last], preferred_element_type=f32),
    )
    for g in range(groups):
        @pl.when((g > first) & (g < last))
        def _():
            inside = (token >= gstart_ref[g]) & (token < gend_ref[g])
            part = jnp.dot(normed_two, cin_ref[g], preferred_element_type=f32)
            hid_scr[...] = jnp.where(inside, part, hid_scr[...])
    hidden = jax.nn.gelu(hid_scr[...]).astype(bf16)
    out_scr[...] = jnp.where(
        head,
        jnp.dot(hidden, cout_ref[first], preferred_element_type=f32),
        jnp.dot(hidden, cout_ref[last], preferred_element_type=f32),
    )
    for g in range(groups):
        @pl.when((g > first) & (g < last))
        def _():
            inside = (token >= gstart_ref[g]) & (token < gend_ref[g])
            part = jnp.dot(hidden, cout_ref[g], preferred_element_type=f32)
            out_scr[...] = jnp.where(inside, part, out_scr[...])
    after_mlp = after_mix + out_scr[...]
    pooled = jnp.mean(after_mlp.reshape(hits, row_len, channels), axis=1).astype(bf16)
    o_ref[...] = jnp.dot(pooled, ro_ref[...], preferred_element_type=f32)


def encode_rows(x, sorted_targets, gstart, gend, tin_all, tout_all, cin_all, cout_all, row_readout):
    hit_count, row_len, channels = x.shape
    steps = hit_count // BLOCK_HITS
    full = lambda a: pl.BlockSpec(a.shape, lambda i, *_: (0,) * a.ndim)
    grid_spec = pltpu.PrefetchScalarGridSpec(
        num_scalar_prefetch=3,
        grid=(steps,),
        in_specs=[
            pl.BlockSpec((BLOCK_HITS, row_len, channels), lambda i, *_: (i, 0, 0)),
            full(tin_all),
            full(tout_all),
            full(cin_all),
            full(cout_all),
            full(row_readout),
        ],
        out_specs=pl.BlockSpec((BLOCK_HITS, channels), lambda i, *_: (i, 0)),
        scratch_shapes=[
            pltpu.VMEM((BLOCK_HITS * row_len, channels), jnp.float32),
            pltpu.VMEM((BLOCK_HITS * row_len, cin_all.shape[-1]), jnp.float32),
            pltpu.VMEM((BLOCK_HITS * row_len, channels), jnp.float32),
        ],
    )
    return pl.pallas_call(
        encoder_kernel,
        grid_spec=grid_spec,
        out_shape=jax.ShapeDtypeStruct((hit_count, channels), jnp.float32),
        compiler_params=pltpu.CompilerParams(dimension_semantics=("arbitrary",)),
    )(sorted_targets, gstart, gend, x, tin_all, tout_all, cin_all, cout_all, row_readout)


def exchange_kernel(n, x_ref, o_ref, recv, send_sems, recv_sems):
    me = lax.axis_index("mod")
    stream = lax.axis_index("stream")
    barrier = pltpu.get_barrier_semaphore()
    for d in range(1, n):
        pl.semaphore_signal(
            barrier, inc=1, device_id=(stream, lax.rem(me + d, n)),
            device_id_type=pl.DeviceIdType.MESH,
        )
    pl.semaphore_wait(barrier, n - 1)
    copies = []
    for d in range(1, n):
        target = lax.rem(me + d, n)
        copy = pltpu.make_async_remote_copy(
            src_ref=x_ref.at[target],
            dst_ref=recv.at[d - 1],
            send_sem=send_sems.at[d - 1],
            recv_sem=recv_sems.at[d - 1],
            device_id=(stream, target),
            device_id_type=pl.DeviceIdType.MESH,
        )
        copy.start()
        copies.append(copy)
    for copy in copies:
        copy.wait()
    total = x_ref[me]
    for d in range(n - 1):
        total = total + recv[d]
    o_ref[...] = total


def exchange_sum(x):
    n = x.shape[0]
    return pl.pallas_call(
        functools.partial(exchange_kernel, n),
        out_shape=jax.ShapeDtypeStruct(x.shape[1:], x.dtype),
        in_specs=[pl.BlockSpec(memory_space=pltpu.VMEM)],
        out_specs=pl.BlockSpec(memory_space=pltpu.VMEM),
        scratch_shapes=[
            pltpu.VMEM((n - 1,) + x.shape[1:], x.dtype),
            pltpu.SemaphoreType.DMA((n - 1,)),
            pltpu.SemaphoreType.DMA((n - 1,)),
        ],
        compiler_params=pltpu.CompilerParams(collective_id=0, has_side_effects=True),
    )(x)


def local(
    pixels,
    stem_weight,
    veto_weight,
    hit_frames,
    assign,
    token_in,
    token_out,
    chan_in,
    chan_out,
    readout,
    latent_gain,
    class_weight,
):
    f32 = jnp.float32
    stream_count = lax.axis_size("stream")
    module_count = lax.axis_size("mod")
    mod_index = lax.axis_index("mod")

    pieces = (token_in[0], token_out[0], chan_in[0], chan_out[0])
    lanes, align = 128, 16
    blocks, spans, start = [], [], 0
    for w in pieces:
        rows = -(-(-(-w.size // lanes)) // align) * align
        blocks.append(jnp.pad(w.reshape(-1), (0, rows * lanes - w.size)).reshape(rows, lanes))
        spans.append((start, rows))
        start += rows
    gathered = lax.all_gather(jnp.concatenate(blocks, axis=0), "stream")
    weights = []
    for w, (first_row, rows) in zip(pieces, spans):
        part = gathered[:, first_row:first_row + rows, :].reshape(stream_count, -1)
        weights.append(part[:, :w.size].reshape((stream_count,) + w.shape))
    tin_all, tout_all, cin_all, cout_all = weights

    features = stem_layer(pixels[0], stem_weight)
    channels = features.shape[-1]
    row_len = features.shape[1]

    means = jnp.mean(features.astype(f32), axis=1)
    row_weight = lax.dynamic_slice_in_dim(veto_weight, mod_index, 1, axis=0)
    veto_part = jnp.sum(means * row_weight, axis=1)

    hits = hit_frames[0]
    targets = assign[0, :, 0].astype(jnp.int32)
    position = jnp.arange(targets.shape[0], dtype=jnp.int32)
    before = (targets[None, :] < targets[:, None]) | (
        (targets[None, :] == targets[:, None]) & (position[None, :] < position[:, None])
    )
    rank = jnp.sum(before.astype(jnp.int32), axis=1)
    picks = rank[None, :] == position[:, None]
    sorted_targets = jnp.sum(jnp.where(picks, targets[None, :], 0), axis=1)
    sorted_frames = jnp.sum(jnp.where(picks, hits[None, :], 0), axis=1)
    x = jnp.take(features, sorted_frames, axis=0)
    counts = jnp.sum(
        (targets[None, :] == jnp.arange(stream_count, dtype=jnp.int32)[:, None]).astype(jnp.int32),
        axis=1,
    )
    gend = jnp.cumsum(counts) * row_len
    gstart = gend - counts * row_len
    row_readout = lax.dynamic_slice_in_dim(readout, mod_index * channels, channels, axis=0)
    projected_sorted = encode_rows(
        x, sorted_targets, gstart.astype(jnp.int32), gend.astype(jnp.int32),
        tin_all, tout_all, cin_all, cout_all, row_readout,
    )
    projected_part = jnp.take(projected_sorted, rank, axis=0)

    packed = jnp.concatenate(
        [
            projected_part.reshape(module_count, -1),
            veto_part.reshape(module_count, -1),
        ],
        axis=1,
    )
    width = packed.shape[1]
    lanes = 128
    padded = -(-width // (8 * lanes)) * 8 * lanes
    packed = jnp.pad(packed, ((0, 0), (0, padded - width)))
    totals = exchange_sum(packed.reshape(module_count, -1, lanes)).reshape(-1)
    split = projected_part.size // module_count
    projected = totals[:split].reshape(-1, channels)
    veto = totals[split:width]
    latent = rms_norm(projected) * latent_gain
    class_scores = jnp.dot(latent, class_weight, precision=lax.Precision.HIGHEST)
    return (veto[None], latent[None], class_scores[None])


def solution(mesh):
    in_specs = (
        P("stream", None, "mod", None),
        P(),
        P(),
        P("stream", None),
        P("stream", None, None),
        P("stream", None, None),
        P("stream", None, None),
        P("stream", None, None),
        P("stream", None, None),
        P(),
        P(),
        P(),
    )
    out_specs = (P("stream", "mod"), P("stream", "mod", None), P("stream", "mod", None))
    return jax.shard_map(local, mesh=mesh, in_specs=in_specs, out_specs=out_specs, check_vma=False)
```

```python
import functools

import jax
import jax.numpy as jnp
from jax import lax
from jax.experimental import pallas as pl
from jax.experimental.pallas import tpu as pltpu
from jax.sharding import PartitionSpec as P

PATCH = 16
BLOCK_HITS = 64


def rms_norm(values):
    return values * lax.rsqrt(jnp.mean(values * values, axis=-1, keepdims=True) + 1e-06)


def stem_layer(frame_pixels, stem_weight):
    count, height, width = frame_pixels.shape
    pixel_tiles = frame_pixels.reshape(count, height // PATCH, PATCH, width // PATCH, PATCH)
    kernel = stem_weight.reshape(PATCH, PATCH, -1)
    response = jnp.einsum(
        "fapbq,pqc->fabc", pixel_tiles, kernel, preferred_element_type=jnp.float32
    )
    return jax.nn.gelu(response).astype(jnp.bfloat16).reshape(count, -1, kernel.shape[-1])


def gelu_tanh(x):
    k = 0.7978845608028654
    inner = x * (k + (k * 0.044715) * (x * x))
    half = 0.5 * x
    return half + half * jnp.tanh(inner)


def encoder_kernel(
    tgt_ref, gstart_ref, gend_ref,
    x_ref, tin_ref, tout_ref, cin_ref, cout_ref, ro_ref,
    o_ref, mix_scr, hid_scr, out_scr,
):
    f32, bf16 = jnp.float32, jnp.bfloat16
    block = pl.program_id(0)
    hits, row_len, channels = x_ref.shape
    groups = cin_ref.shape[0]
    base = block * hits
    for h in range(hits):
        t = tgt_ref[base + h]
        xh = x_ref[h].astype(f32)
        normed = rms_norm(xh).astype(bf16)
        pre = jnp.dot(tin_ref[t], normed, preferred_element_type=f32)
        mixed = gelu_tanh(pre.astype(bf16)).astype(bf16)
        mix = jnp.dot(tout_ref[t], mixed, preferred_element_type=f32)
        mix_scr[h * row_len:(h + 1) * row_len, :] = (xh + mix).astype(bf16).astype(f32)
    after_mix = mix_scr[...]
    normed_two = rms_norm(after_mix).astype(bf16)
    token = base * row_len + lax.broadcasted_iota(jnp.int32, (hits * row_len, 1), 0)
    first = tgt_ref[base]
    last = tgt_ref[base + hits - 1]
    head = token < gend_ref[first]
    hid_scr[...] = jnp.where(
        head,
        jnp.dot(normed_two, cin_ref[first], preferred_element_type=f32),
        jnp.dot(normed_two, cin_ref[last], preferred_element_type=f32),
    )
    for g in range(groups):
        @pl.when((g > first) & (g < last))
        def _():
            inside = (token >= gstart_ref[g]) & (token < gend_ref[g])
            part = jnp.dot(normed_two, cin_ref[g], preferred_element_type=f32)
            hid_scr[...] = jnp.where(inside, part, hid_scr[...])
    hidden = jax.nn.gelu(hid_scr[...]).astype(bf16)
    out_scr[...] = jnp.where(
        head,
        jnp.dot(hidden, cout_ref[first], preferred_element_type=f32),
        jnp.dot(hidden, cout_ref[last], preferred_element_type=f32),
    )
    for g in range(groups):
        @pl.when((g > first) & (g < last))
        def _():
            inside = (token >= gstart_ref[g]) & (token < gend_ref[g])
            part = jnp.dot(hidden, cout_ref[g], preferred_element_type=f32)
            out_scr[...] = jnp.where(inside, part, out_scr[...])
    after_mlp = after_mix + out_scr[...]
    pooled = jnp.mean(after_mlp.reshape(hits, row_len, channels), axis=1).astype(bf16)
    o_ref[...] = jnp.dot(pooled, ro_ref[...], preferred_element_type=f32)


def encode_rows(x, sorted_targets, gstart, gend, tin_all, tout_all, cin_all, cout_all, row_readout):
    hit_count, row_len, channels = x.shape
    steps = hit_count // BLOCK_HITS
    full = lambda a: pl.BlockSpec(a.shape, lambda i, *_: (0,) * a.ndim)
    grid_spec = pltpu.PrefetchScalarGridSpec(
        num_scalar_prefetch=3,
        grid=(steps,),
        in_specs=[
            pl.BlockSpec((BLOCK_HITS, row_len, channels), lambda i, *_: (i, 0, 0)),
            full(tin_all),
            full(tout_all),
            full(cin_all),
            full(cout_all),
            full(row_readout),
        ],
        out_specs=pl.BlockSpec((BLOCK_HITS, channels), lambda i, *_: (i, 0)),
        scratch_shapes=[
            pltpu.VMEM((BLOCK_HITS * row_len, channels), jnp.float32),
            pltpu.VMEM((BLOCK_HITS * row_len, cin_all.shape[-1]), jnp.float32),
            pltpu.VMEM((BLOCK_HITS * row_len, channels), jnp.float32),
        ],
    )
    return pl.pallas_call(
        encoder_kernel,
        grid_spec=grid_spec,
        out_shape=jax.ShapeDtypeStruct((hit_count, channels), jnp.float32),
        compiler_params=pltpu.CompilerParams(dimension_semantics=("arbitrary",)),
    )(sorted_targets, gstart, gend, x, tin_all, tout_all, cin_all, cout_all, row_readout)


def exchange_kernel(n, x_ref, o_ref, recv, send_sems, recv_sems):
    me = lax.axis_index("mod")
    stream = lax.axis_index("stream")
    barrier = pltpu.get_barrier_semaphore()
    for d in range(1, n):
        pl.semaphore_signal(
            barrier, inc=1, device_id=(stream, lax.rem(me + d, n)),
            device_id_type=pl.DeviceIdType.MESH,
        )
    pl.semaphore_wait(barrier, n - 1)
    copies = []
    for d in range(1, n):
        target = lax.rem(me + d, n)
        copy = pltpu.make_async_remote_copy(
            src_ref=x_ref.at[target],
            dst_ref=recv.at[d - 1],
            send_sem=send_sems.at[d - 1],
            recv_sem=recv_sems.at[d - 1],
            device_id=(stream, target),
            device_id_type=pl.DeviceIdType.MESH,
        )
        copy.start()
        copies.append(copy)
    for copy in copies:
        copy.wait()
    total = x_ref[me]
    for d in range(n - 1):
        total = total + recv[d]
    o_ref[...] = total


def exchange_sum(x):
    n = x.shape[0]
    return pl.pallas_call(
        functools.partial(exchange_kernel, n),
        out_shape=jax.ShapeDtypeStruct(x.shape[1:], x.dtype),
        in_specs=[pl.BlockSpec(memory_space=pltpu.VMEM)],
        out_specs=pl.BlockSpec(memory_space=pltpu.VMEM),
        scratch_shapes=[
            pltpu.VMEM((n - 1,) + x.shape[1:], x.dtype),
            pltpu.SemaphoreType.DMA((n - 1,)),
            pltpu.SemaphoreType.DMA((n - 1,)),
        ],
        compiler_params=pltpu.CompilerParams(collective_id=0, has_side_effects=True),
    )(x)


def local(
    pixels,
    stem_weight,
    veto_weight,
    hit_frames,
    assign,
    token_in,
    token_out,
    chan_in,
    chan_out,
    readout,
    latent_gain,
    class_weight,
):
    f32 = jnp.float32
    stream_count = lax.axis_size("stream")
    module_count = lax.axis_size("mod")
    mod_index = lax.axis_index("mod")

    pieces = (token_in[0], token_out[0], chan_in[0], chan_out[0])
    lanes, align = 128, 16
    blocks, spans, start = [], [], 0
    for w in pieces:
        rows = -(-(-(-w.size // lanes)) // align) * align
        blocks.append(jnp.pad(w.reshape(-1), (0, rows * lanes - w.size)).reshape(rows, lanes))
        spans.append((start, rows))
        start += rows
    gathered = lax.all_gather(jnp.concatenate(blocks, axis=0), "stream")
    weights = []
    for w, (first_row, rows) in zip(pieces, spans):
        part = gathered[:, first_row:first_row + rows, :].reshape(stream_count, -1)
        weights.append(part[:, :w.size].reshape((stream_count,) + w.shape))
    tin_all, tout_all, cin_all, cout_all = weights

    features = stem_layer(pixels[0], stem_weight)
    channels = features.shape[-1]
    row_len = features.shape[1]

    means = jnp.mean(features.astype(f32), axis=1)
    row_weight = lax.dynamic_slice_in_dim(veto_weight, mod_index, 1, axis=0)
    veto_part = jnp.sum(means * row_weight, axis=1)

    hits = hit_frames[0]
    targets = assign[0, :, 0].astype(jnp.int32)
    position = jnp.arange(targets.shape[0], dtype=jnp.int32)
    before = (targets[None, :] < targets[:, None]) | (
        (targets[None, :] == targets[:, None]) & (position[None, :] < position[:, None])
    )
    rank = jnp.sum(before.astype(jnp.int32), axis=1)
    picks = rank[None, :] == position[:, None]
    sorted_targets = jnp.sum(jnp.where(picks, targets[None, :], 0), axis=1)
    sorted_frames = jnp.sum(jnp.where(picks, hits[None, :], 0), axis=1)
    x = jnp.take(features, sorted_frames, axis=0)
    counts = jnp.sum(
        (targets[None, :] == jnp.arange(stream_count, dtype=jnp.int32)[:, None]).astype(jnp.int32),
        axis=1,
    )
    gend = jnp.cumsum(counts) * row_len
    gstart = gend - counts * row_len
    row_readout = lax.dynamic_slice_in_dim(readout, mod_index * channels, channels, axis=0)
    projected_sorted = encode_rows(
        x, sorted_targets, gstart.astype(jnp.int32), gend.astype(jnp.int32),
        tin_all, tout_all, cin_all, cout_all, row_readout,
    )
    projected_part = jnp.take(projected_sorted, rank, axis=0)

    packed = jnp.concatenate(
        [
            projected_part.reshape(module_count, -1),
            veto_part.reshape(module_count, -1),
        ],
        axis=1,
    )
    width = packed.shape[1]
    lanes = 128
    padded = -(-width // (8 * lanes)) * 8 * lanes
    packed = jnp.pad(packed, ((0, 0), (0, padded - width)))
    totals = exchange_sum(packed.reshape(module_count, -1, lanes)).reshape(-1)
    split = projected_part.size // module_count
    projected = totals[:split].reshape(-1, channels)
    veto = totals[split:width]
    latent = rms_norm(projected) * latent_gain
    class_scores = jnp.dot(latent, class_weight, precision=lax.Precision.HIGHEST)
    return (veto[None], latent[None], class_scores[None])


def solution(mesh):
    in_specs = (
        P("stream", None, "mod", None),
        P(),
        P(),
        P("stream", None),
        P("stream", None, None),
        P("stream", None, None),
        P("stream", None, None),
        P("stream", None, None),
        P("stream", None, None),
        P(),
        P(),
        P(),
    )
    out_specs = (P("stream", "mod"), P("stream", "mod", None), P("stream", "mod", None))
    return jax.shard_map(local, mesh=mesh, in_specs=in_specs, out_specs=out_specs, check_vma=False)
```

```python
import functools

import jax
import jax.numpy as jnp
from jax import lax
from jax.experimental import pallas as pl
from jax.experimental.pallas import tpu as pltpu
from jax.sharding import PartitionSpec as P

PATCH = 16
BLOCK_HITS = 32


def rms_norm(values):
    return values * lax.rsqrt(jnp.mean(values * values, axis=-1, keepdims=True) + 1e-06)


def stem_layer(frame_pixels, stem_weight):
    count, height, width = frame_pixels.shape
    pixel_tiles = frame_pixels.reshape(count, height // PATCH, PATCH, width // PATCH, PATCH)
    kernel = stem_weight.reshape(PATCH, PATCH, -1)
    response = jnp.einsum(
        "fapbq,pqc->fabc", pixel_tiles, kernel, preferred_element_type=jnp.float32
    )
    return jax.nn.gelu(response).astype(jnp.bfloat16).reshape(count, -1, kernel.shape[-1])


def gelu_tanh(x):
    k = 0.7978845608028654
    inner = x * (k + (k * 0.044715) * (x * x))
    half = 0.5 * x
    return half + half * jnp.tanh(inner)


def encoder_kernel(
    tgt_ref, gstart_ref, gend_ref, order_ref,
    x_ref, tin_ref, tout_ref, cin_ref, cout_ref, ro_ref,
    o_ref, mix_scr, hid_scr, out_scr,
):
    f32, bf16 = jnp.float32, jnp.bfloat16
    block = pl.program_id(0)
    hits, row_len, channels = x_ref.shape
    groups = cin_ref.shape[0]
    base = block * hits
    for h in range(hits):
        t = tgt_ref[base + h]
        xh = x_ref[h].astype(f32)
        normed = rms_norm(xh).astype(bf16)
        pre = jnp.dot(tin_ref[t], normed, preferred_element_type=f32)
        mixed = gelu_tanh(pre.astype(bf16)).astype(bf16)
        mix = jnp.dot(tout_ref[t], mixed, preferred_element_type=f32)
        mix_scr[h * row_len:(h + 1) * row_len, :] = (xh + mix).astype(bf16).astype(f32)
    after_mix = mix_scr[...]
    normed_two = rms_norm(after_mix).astype(bf16)
    token = base * row_len + lax.broadcasted_iota(jnp.int32, (hits * row_len, 1), 0)
    first = tgt_ref[base]
    last = tgt_ref[base + hits - 1]
    head = token < gend_ref[first]
    hid_scr[...] = jnp.where(
        head,
        jnp.dot(normed_two, cin_ref[first], preferred_element_type=f32),
        jnp.dot(normed_two, cin_ref[last], preferred_element_type=f32),
    )
    for g in range(groups):
        @pl.when((g > first) & (g < last))
        def _():
            inside = (token >= gstart_ref[g]) & (token < gend_ref[g])
            part = jnp.dot(normed_two, cin_ref[g], preferred_element_type=f32)
            hid_scr[...] = jnp.where(inside, part, hid_scr[...])
    hidden = jax.nn.gelu(hid_scr[...]).astype(bf16)
    out_scr[...] = jnp.where(
        head,
        jnp.dot(hidden, cout_ref[first], preferred_element_type=f32),
        jnp.dot(hidden, cout_ref[last], preferred_element_type=f32),
    )
    for g in range(groups):
        @pl.when((g > first) & (g < last))
        def _():
            inside = (token >= gstart_ref[g]) & (token < gend_ref[g])
            part = jnp.dot(hidden, cout_ref[g], preferred_element_type=f32)
            out_scr[...] = jnp.where(inside, part, out_scr[...])
    after_mlp = after_mix + out_scr[...]
    pooled = jnp.mean(after_mlp.reshape(hits, row_len, channels), axis=1).astype(bf16)
    projected = jnp.dot(pooled, ro_ref[...], preferred_element_type=f32)

    @pl.when(block == 0)
    def _():
        o_ref[...] = jnp.zeros_like(o_ref)

    per_owner = order_ref.shape[0] // o_ref.shape[0]
    for h in range(hits):
        hit = order_ref[base + h]
        o_ref[hit // per_owner, pl.ds(hit % per_owner, 1), :] = projected[h:h + 1, :]


def encode_rows(x, sorted_targets, gstart, gend, order, owners, tin_all, tout_all, cin_all, cout_all, row_readout):
    hit_count, row_len, channels = x.shape
    steps = hit_count // BLOCK_HITS
    full = lambda a: pl.BlockSpec(a.shape, lambda i, *_: (0,) * a.ndim)
    grid_spec = pltpu.PrefetchScalarGridSpec(
        num_scalar_prefetch=4,
        grid=(steps,),
        in_specs=[
            pl.BlockSpec((BLOCK_HITS, row_len, channels), lambda i, *_: (i, 0, 0)),
            full(tin_all),
            full(tout_all),
            full(cin_all),
            full(cout_all),
            full(row_readout),
        ],
        out_specs=pl.BlockSpec((owners, 8, channels), lambda i, *_: (0, 0, 0)),
        scratch_shapes=[
            pltpu.VMEM((BLOCK_HITS * row_len, channels), jnp.float32),
            pltpu.VMEM((BLOCK_HITS * row_len, cin_all.shape[-1]), jnp.float32),
            pltpu.VMEM((BLOCK_HITS * row_len, channels), jnp.float32),
        ],
    )
    return pl.pallas_call(
        encoder_kernel,
        grid_spec=grid_spec,
        out_shape=jax.ShapeDtypeStruct((owners, 8, channels), jnp.float32),
        compiler_params=pltpu.CompilerParams(dimension_semantics=("arbitrary",)),
    )(sorted_targets, gstart, gend, order, x, tin_all, tout_all, cin_all, cout_all, row_readout)


def exchange_kernel(n, x_ref, o_ref, recv, send_sems, recv_sems):
    me = lax.axis_index("mod")
    stream = lax.axis_index("stream")
    barrier = pltpu.get_barrier_semaphore()
    for d in range(1, n):
        pl.semaphore_signal(
            barrier, inc=1, device_id=(stream, lax.rem(me + d, n)),
            device_id_type=pl.DeviceIdType.MESH,
        )
    pl.semaphore_wait(barrier, n - 1)
    copies = []
    for d in range(1, n):
        target = lax.rem(me + d, n)
        copy = pltpu.make_async_remote_copy(
            src_ref=x_ref.at[target],
            dst_ref=recv.at[d - 1],
            send_sem=send_sems.at[d - 1],
            recv_sem=recv_sems.at[d - 1],
            device_id=(stream, target),
            device_id_type=pl.DeviceIdType.MESH,
        )
        copy.start()
        copies.append(copy)
    for copy in copies:
        copy.wait()
    total = x_ref[me]
    for d in range(n - 1):
        total = total + recv[d]
    o_ref[...] = total


def exchange_sum(x):
    n = x.shape[0]
    return pl.pallas_call(
        functools.partial(exchange_kernel, n),
        out_shape=jax.ShapeDtypeStruct(x.shape[1:], x.dtype),
        in_specs=[pl.BlockSpec(memory_space=pltpu.VMEM)],
        out_specs=pl.BlockSpec(memory_space=pltpu.VMEM),
        scratch_shapes=[
            pltpu.VMEM((n - 1,) + x.shape[1:], x.dtype),
            pltpu.SemaphoreType.DMA((n - 1,)),
            pltpu.SemaphoreType.DMA((n - 1,)),
        ],
        compiler_params=pltpu.CompilerParams(collective_id=0, has_side_effects=True),
    )(x)


def local(
    pixels,
    stem_weight,
    veto_weight,
    hit_frames,
    assign,
    token_in,
    token_out,
    chan_in,
    chan_out,
    readout,
    latent_gain,
    class_weight,
):
    f32 = jnp.float32
    stream_count = lax.axis_size("stream")
    module_count = lax.axis_size("mod")
    mod_index = lax.axis_index("mod")

    pieces = (token_in[0], token_out[0], chan_in[0], chan_out[0])
    lanes, align = 128, 16
    blocks, spans, start = [], [], 0
    for w in pieces:
        rows = -(-(-(-w.size // lanes)) // align) * align
        blocks.append(jnp.pad(w.reshape(-1), (0, rows * lanes - w.size)).reshape(rows, lanes))
        spans.append((start, rows))
        start += rows
    gathered = lax.all_gather(jnp.concatenate(blocks, axis=0), "stream")
    weights = []
    for w, (first_row, rows) in zip(pieces, spans):
        part = gathered[:, first_row:first_row + rows, :].reshape(stream_count, -1)
        weights.append(part[:, :w.size].reshape((stream_count,) + w.shape))
    tin_all, tout_all, cin_all, cout_all = weights

    features = stem_layer(pixels[0], stem_weight)
    channels = features.shape[-1]
    row_len = features.shape[1]

    means = jnp.mean(features.astype(f32), axis=1)
    row_weight = lax.dynamic_slice_in_dim(veto_weight, mod_index, 1, axis=0)
    veto_part = jnp.sum(means * row_weight, axis=1)

    hits = hit_frames[0]
    targets = assign[0, :, 0].astype(jnp.int32)
    position = jnp.arange(targets.shape[0], dtype=jnp.int32)
    before = (targets[None, :] < targets[:, None]) | (
        (targets[None, :] == targets[:, None]) & (position[None, :] < position[:, None])
    )
    rank = jnp.sum(before.astype(jnp.int32), axis=1)
    picks = rank[None, :] == position[:, None]
    sorted_targets = jnp.sum(jnp.where(picks, targets[None, :], 0), axis=1)
    sorted_frames = jnp.sum(jnp.where(picks, hits[None, :], 0), axis=1)
    x = jnp.take(features, sorted_frames, axis=0)
    counts = jnp.sum(
        (targets[None, :] == jnp.arange(stream_count, dtype=jnp.int32)[:, None]).astype(jnp.int32),
        axis=1,
    )
    gend = jnp.cumsum(counts) * row_len
    gstart = gend - counts * row_len
    row_readout = lax.dynamic_slice_in_dim(readout, mod_index * channels, channels, axis=0)
    order = jnp.sum(jnp.where(picks, position[None, :], 0), axis=1)
    hits_per_owner = targets.shape[0] // module_count
    packed = encode_rows(
        x, sorted_targets, gstart.astype(jnp.int32), gend.astype(jnp.int32),
        order.astype(jnp.int32), module_count,
        tin_all, tout_all, cin_all, cout_all, row_readout,
    )
    veto_rows = veto_part.reshape(module_count, 1, -1)
    packed = lax.dynamic_update_slice(packed, veto_rows, (0, hits_per_owner, 0))
    lanes = 128
    split = hits_per_owner * channels
    width = split + veto_rows.shape[-1]
    totals = exchange_sum(packed).reshape(-1)
    projected = totals[:split].reshape(-1, channels)
    veto = totals[split:width]
    latent = rms_norm(projected) * latent_gain
    class_scores = jnp.dot(latent, class_weight, precision=lax.Precision.HIGHEST)
    return (veto[None], latent[None], class_scores[None])


def solution(mesh):
    in_specs = (
        P("stream", None, "mod", None),
        P(),
        P(),
        P("stream", None),
        P("stream", None, None),
        P("stream", None, None),
        P("stream", None, None),
        P("stream", None, None),
        P("stream", None, None),
        P(),
        P(),
        P(),
    )
    out_specs = (P("stream", "mod"), P("stream", "mod", None), P("stream", "mod", None))
    return jax.shard_map(local, mesh=mesh, in_specs=in_specs, out_specs=out_specs, check_vma=False)
```

```python
import functools

import jax
import jax.numpy as jnp
from jax import lax
from jax.experimental import pallas as pl
from jax.experimental.pallas import tpu as pltpu
from jax.sharding import PartitionSpec as P

PATCH = 16
BLOCK_HITS = 24


def rms_norm(values):
    return values * lax.rsqrt(jnp.mean(values * values, axis=-1, keepdims=True) + 1e-06)


def stem_layer(frame_pixels, stem_weight):
    count, height, width = frame_pixels.shape
    pixel_tiles = frame_pixels.reshape(count, height // PATCH, PATCH, width // PATCH, PATCH)
    kernel = stem_weight.reshape(PATCH, PATCH, -1)
    response = jnp.einsum(
        "fapbq,pqc->fabc", pixel_tiles, kernel, preferred_element_type=jnp.float32
    )
    return jax.nn.gelu(response).astype(jnp.bfloat16).reshape(count, -1, kernel.shape[-1])


def gelu_tanh(x):
    k = 0.7978845608028654
    inner = x * (k + (k * 0.044715) * (x * x))
    half = 0.5 * x
    return half + half * jnp.tanh(inner)


def encoder_kernel(
    tgt_ref, gstart_ref, gend_ref,
    x_ref, tin_ref, tout_ref, cin_ref, cout_ref, ro_ref,
    o_ref, mix_scr, hid_scr, out_scr,
):
    f32, bf16 = jnp.float32, jnp.bfloat16
    block = pl.program_id(0)
    hits, row_len, channels = x_ref.shape
    groups = cin_ref.shape[0]
    base = block * hits
    for h in range(hits):
        t = tgt_ref[base + h]
        xh = x_ref[h].astype(f32)
        normed = rms_norm(xh).astype(bf16)
        pre = jnp.dot(tin_ref[t], normed, preferred_element_type=f32)
        mixed = gelu_tanh(pre.astype(bf16)).astype(bf16)
        mix = jnp.dot(tout_ref[t], mixed, preferred_element_type=f32)
        mix_scr[h * row_len:(h + 1) * row_len, :] = (xh + mix).astype(bf16).astype(f32)
    after_mix = mix_scr[...]
    normed_two = rms_norm(after_mix).astype(bf16)
    token = base * row_len + lax.broadcasted_iota(jnp.int32, (hits * row_len, 1), 0)
    first = tgt_ref[base]
    last = tgt_ref[base + hits - 1]
    head = token < gend_ref[first]
    hid_scr[...] = jnp.where(
        head,
        jnp.dot(normed_two, cin_ref[first], preferred_element_type=f32),
        jnp.dot(normed_two, cin_ref[last], preferred_element_type=f32),
    )
    for g in range(groups):
        @pl.when((g > first) & (g < last))
        def _():
            inside = (token >= gstart_ref[g]) & (token < gend_ref[g])
            part = jnp.dot(normed_two, cin_ref[g], preferred_element_type=f32)
            hid_scr[...] = jnp.where(inside, part, hid_scr[...])
    hidden = jax.nn.gelu(hid_scr[...]).astype(bf16)
    out_scr[...] = jnp.where(
        head,
        jnp.dot(hidden, cout_ref[first], preferred_element_type=f32),
        jnp.dot(hidden, cout_ref[last], preferred_element_type=f32),
    )
    for g in range(groups):
        @pl.when((g > first) & (g < last))
        def _():
            inside = (token >= gstart_ref[g]) & (token < gend_ref[g])
            part = jnp.dot(hidden, cout_ref[g], preferred_element_type=f32)
            out_scr[...] = jnp.where(inside, part, out_scr[...])
    after_mlp = after_mix + out_scr[...]
    pooled = jnp.mean(after_mlp.reshape(hits, row_len, channels), axis=1).astype(bf16)
    o_ref[...] = jnp.dot(pooled, ro_ref[...], preferred_element_type=f32)


def encode_rows(x, sorted_targets, gstart, gend, tin_all, tout_all, cin_all, cout_all, row_readout):
    hit_count, row_len, channels = x.shape
    steps = hit_count // BLOCK_HITS
    full = lambda a: pl.BlockSpec(a.shape, lambda i, *_: (0,) * a.ndim)
    grid_spec = pltpu.PrefetchScalarGridSpec(
        num_scalar_prefetch=3,
        grid=(steps,),
        in_specs=[
            pl.BlockSpec((BLOCK_HITS, row_len, channels), lambda i, *_: (i, 0, 0)),
            full(tin_all),
            full(tout_all),
            full(cin_all),
            full(cout_all),
            full(row_readout),
        ],
        out_specs=pl.BlockSpec((BLOCK_HITS, channels), lambda i, *_: (i, 0)),
        scratch_shapes=[
            pltpu.VMEM((BLOCK_HITS * row_len, channels), jnp.float32),
            pltpu.VMEM((BLOCK_HITS * row_len, cin_all.shape[-1]), jnp.float32),
            pltpu.VMEM((BLOCK_HITS * row_len, channels), jnp.float32),
        ],
    )
    return pl.pallas_call(
        encoder_kernel,
        grid_spec=grid_spec,
        out_shape=jax.ShapeDtypeStruct((hit_count, channels), jnp.float32),
        compiler_params=pltpu.CompilerParams(dimension_semantics=("arbitrary",)),
    )(sorted_targets, gstart, gend, x, tin_all, tout_all, cin_all, cout_all, row_readout)


def exchange_kernel(n, x_ref, o_ref, recv, send_sems, recv_sems):
    me = lax.axis_index("mod")
    stream = lax.axis_index("stream")
    barrier = pltpu.get_barrier_semaphore()
    for d in range(1, n):
        pl.semaphore_signal(
            barrier, inc=1, device_id=(stream, lax.rem(me + d, n)),
            device_id_type=pl.DeviceIdType.MESH,
        )
    pl.semaphore_wait(barrier, n - 1)
    copies = []
    for d in range(1, n):
        target = lax.rem(me + d, n)
        copy = pltpu.make_async_remote_copy(
            src_ref=x_ref.at[target],
            dst_ref=recv.at[d - 1],
            send_sem=send_sems.at[d - 1],
            recv_sem=recv_sems.at[d - 1],
            device_id=(stream, target),
            device_id_type=pl.DeviceIdType.MESH,
        )
        copy.start()
        copies.append(copy)
    for copy in copies:
        copy.wait()
    total = x_ref[me]
    for d in range(n - 1):
        total = total + recv[d]
    o_ref[...] = total


def exchange_sum(x):
    n = x.shape[0]
    return pl.pallas_call(
        functools.partial(exchange_kernel, n),
        out_shape=jax.ShapeDtypeStruct(x.shape[1:], x.dtype),
        in_specs=[pl.BlockSpec(memory_space=pltpu.VMEM)],
        out_specs=pl.BlockSpec(memory_space=pltpu.VMEM),
        scratch_shapes=[
            pltpu.VMEM((n - 1,) + x.shape[1:], x.dtype),
            pltpu.SemaphoreType.DMA((n - 1,)),
            pltpu.SemaphoreType.DMA((n - 1,)),
        ],
        compiler_params=pltpu.CompilerParams(collective_id=0, has_side_effects=True),
    )(x)


def local(
    pixels,
    stem_weight,
    veto_weight,
    hit_frames,
    assign,
    token_in,
    token_out,
    chan_in,
    chan_out,
    readout,
    latent_gain,
    class_weight,
):
    f32 = jnp.float32
    stream_count = lax.axis_size("stream")
    module_count = lax.axis_size("mod")
    mod_index = lax.axis_index("mod")

    pieces = (token_in[0], token_out[0], chan_in[0], chan_out[0])
    lanes, align = 128, 16
    blocks, spans, start = [], [], 0
    for w in pieces:
        rows = -(-(-(-w.size // lanes)) // align) * align
        blocks.append(jnp.pad(w.reshape(-1), (0, rows * lanes - w.size)).reshape(rows, lanes))
        spans.append((start, rows))
        start += rows
    gathered = lax.all_gather(jnp.concatenate(blocks, axis=0), "stream")
    weights = []
    for w, (first_row, rows) in zip(pieces, spans):
        part = gathered[:, first_row:first_row + rows, :].reshape(stream_count, -1)
        weights.append(part[:, :w.size].reshape((stream_count,) + w.shape))
    tin_all, tout_all, cin_all, cout_all = weights

    features = stem_layer(pixels[0], stem_weight)
    channels = features.shape[-1]
    row_len = features.shape[1]

    means = jnp.mean(features.astype(f32), axis=1)
    row_weight = lax.dynamic_slice_in_dim(veto_weight, mod_index, 1, axis=0)
    veto_part = jnp.sum(means * row_weight, axis=1)

    hits = hit_frames[0]
    targets = assign[0, :, 0].astype(jnp.int32)
    position = jnp.arange(targets.shape[0], dtype=jnp.int32)
    before = (targets[None, :] < targets[:, None]) | (
        (targets[None, :] == targets[:, None]) & (position[None, :] < position[:, None])
    )
    rank = jnp.sum(before.astype(jnp.int32), axis=1)
    picks = rank[None, :] == position[:, None]
    sorted_targets = jnp.sum(jnp.where(picks, targets[None, :], 0), axis=1)
    sorted_frames = jnp.sum(jnp.where(picks, hits[None, :], 0), axis=1)
    x = jnp.take(features, sorted_frames, axis=0)
    counts = jnp.sum(
        (targets[None, :] == jnp.arange(stream_count, dtype=jnp.int32)[:, None]).astype(jnp.int32),
        axis=1,
    )
    gend = jnp.cumsum(counts) * row_len
    gstart = gend - counts * row_len
    row_readout = lax.dynamic_slice_in_dim(readout, mod_index * channels, channels, axis=0)
    projected_sorted = encode_rows(
        x, sorted_targets, gstart.astype(jnp.int32), gend.astype(jnp.int32),
        tin_all, tout_all, cin_all, cout_all, row_readout,
    )
    projected_part = jnp.take(projected_sorted, rank, axis=0)

    packed = jnp.concatenate(
        [
            projected_part.reshape(module_count, -1),
            veto_part.reshape(module_count, -1),
        ],
        axis=1,
    )
    width = packed.shape[1]
    lanes = 128
    padded = -(-width // (8 * lanes)) * 8 * lanes
    packed = jnp.pad(packed, ((0, 0), (0, padded - width)))
    totals = exchange_sum(packed.reshape(module_count, -1, lanes)).reshape(-1)
    split = projected_part.size // module_count
    projected = totals[:split].reshape(-1, channels)
    veto = totals[split:width]
    latent = rms_norm(projected) * latent_gain
    class_scores = jnp.dot(latent, class_weight, precision=lax.Precision.HIGHEST)
    return (veto[None], latent[None], class_scores[None])


def solution(mesh):
    in_specs = (
        P("stream", None, "mod", None),
        P(),
        P(),
        P("stream", None),
        P("stream", None, None),
        P("stream", None, None),
        P("stream", None, None),
        P("stream", None, None),
        P("stream", None, None),
        P(),
        P(),
        P(),
    )
    out_specs = (P("stream", "mod"), P("stream", "mod", None), P("stream", "mod", None))
    return jax.shard_map(local, mesh=mesh, in_specs=in_specs, out_specs=out_specs, check_vma=False)
```
